512 devices in a mesh: az: 32 (over z, x), ax: 16 (over y, core).
Axes of the slice: x: 4, y: 8, z: 8, core: 2. Of those that a mesh axis runs over, the one named last changes fastest.
Arguments:
- state: float32 [24576, 5, 512], P(('az', 'ax')), may hold values from -6 to 6
- velocity: float32 [24576, 3], P(('az', 'ax')), may hold values from -4 to 4
- interp_maps: float32 [24576, 3, 8, 8], P(('az', 'ax')), may hold values from -2 to 2
- neighbours: int32 [24576, 6], P(('az', 'ax')), may hold values from 0 to 1055
- send_faces: int32 [24576], P(('az', 'ax')), may hold values from 0 to 287
- owner_device: int32 [24576, 1], P(('az', 'ax')), may hold values from 0 to 31; in each aligned block of 48 rows (0 to 47, 48 to 95, ...) at most 3 rows name the same one
- owner_block: int32 [24576], P(('az', 'ax')), may hold values from 0 to 7
Outputs:
- new_state: float32 [24576, 5, 512], P(('az', 'ax'))
- spectrum: float32 [2, 5, 4096, 512], P(None, None, ('az', 'ax'))
The draws below stay inside these ranges and needn't reach their ends.
Inputs may be any that keep to these rules, and one draw needn't show every extreme that they name: `owner_device`: in the rows of one device at most 3 elements name the same owner sector, and 3 is reached in some device.
All inputs are finite; a program needn't handle non-finite values.
Results may differ from the reference program's by a relative error of at most 0.0003.
Values sent between devices are 32-bit elements; how exact they have to be, the bound alone decides.
A program may use at most 64 MiB of HBM per device.

```python
import math
import jax
import jax.numpy as jnp
import numpy as np
from jax import lax

E_DEV = 48
TB = 2
PB = 4
CB_DEV = 8
CAP = 3
E_TOTAL = 24576
NTH = 512
CYCLE_DEV = 8
CYCLES = 4096
FACE_SLOTS = 1056
N_AZ = 32
N_AX = 16


def plant(array, rng, smallest, high):
    longest = array.shape.index(max(array.shape))
    spots = []
    for shift in (0, 1):
        where = [jax.random.randint(jax.random.fold_in(rng, axis), (), 0, length) for axis, length in enumerate(array.shape)]
        where[longest] = (where[longest] + shift) % array.shape[longest]
        spots.append(tuple(where))
    return array.at[spots[0]].set(smallest).at[spots[1]].set(high)


def block_levels(rng, extent, shards, least, high):
    gain = 1.0
    for axis_at, shards_of in shards:
        steps = jax.random.uniform(jax.random.fold_in(jax.random.fold_in(rng, 6), axis_at), (shards_of,), jnp.float32, least / len(shards), high / len(shards))
        gain = gain * jnp.repeat(jnp.exp(steps), extent[axis_at] // shards_of).reshape((-1,) + (1,) * (len(extent) - 1 - axis_at))
    return gain


def deal_out(key, own, number, rows, number_of, top, reach, skew):
    order = jax.random.permutation(key, number_of)
    crowded, usual = shares(number_of, rows * top, reach, skew, True), shares(number_of, rows * top, reach, skew, False)
    places = jnp.arange(number_of)

    def named(lengths, offset_by):
        used = int((lengths > 0).sum())
        fixed = max(1, used // 4)
        moved = fixed + (places - fixed + offset_by * (used - fixed)) % max(1, number_of - fixed)
        return jnp.zeros((number_of,), jnp.int32).at[order[jnp.where(places < fixed, places, moved)]].set(jnp.asarray(lengths, jnp.int32))

    lengths = jnp.where(number % 4 == 0, named(crowded, number // 4), named(usual, number - number // 4 - 1))
    mixed = jax.random.permutation(jax.random.fold_in(own, 3), number_of)
    source_of, sink = mixed[0:number_of // 2 * 2:2], mixed[1:number_of // 2 * 2:2]
    margin = jnp.minimum(lengths[source_of] - 1, reach - lengths[sink]) // 2
    margin = jnp.where((source_of == order[0]) | (sink == order[0]) | (lengths[sink] == 0), 0, jnp.maximum(margin, 0))
    moved = jax.random.randint(jax.random.fold_in(own, 4), (number_of // 2,), 0, 1 << 20) % (margin + 1)
    lengths = lengths.at[source_of].add(-moved).at[sink].add(moved)
    labels = jnp.searchsorted(jnp.cumsum(lengths), jnp.arange(rows * top), side="right").astype(jnp.int32)
    grid = labels.reshape(top, rows).T
    grid = grid[jax.random.permutation(jax.random.fold_in(own, 1), rows)]
    offset_by = jax.random.randint(jax.random.fold_in(own, 2), (rows, 1), 0, top)
    return jnp.take_along_axis(grid, (jnp.arange(top)[None, :] + offset_by) % top, axis=1)


def shares(amount, total, bound, skew, full):
    loads = [(1 << 20) // math.isqrt(grade ** skew) + 1 for grade in range(1, amount + 1)]
    largest = bound if full else min(bound, max(-(-total // amount), total * loads[0] // sum(loads)))
    least = 1 if total - largest >= amount - 1 else 0
    counts, rest = [largest] + [least] * (amount - 1), total - largest - least * (amount - 1)
    while rest > 0:
        candidates = [i for i in range(1, amount) if counts[i] < largest] or [i for i in range(1, amount) if counts[i] < bound]
        whole, left = sum([loads[i] for i in candidates]), rest
        for i in candidates:
            more = min(bound - counts[i], max(1, left * loads[i] // whole), rest)
            counts[i] = counts[i] + more
            rest = rest - more
    return np.array(counts)


def scatter_about(rng, dims, scale, limit, shards=(), kind=jnp.bfloat16):
    drawn = jax.random.normal(rng, dims, jnp.float32) * scale
    if len(shards) > 0:
        drawn = block_levels(rng, dims, shards, -0.22, 0.18) * drawn
    return jnp.clip(drawn, min=-limit, max=limit).astype(kind)


def setup_inputs(seed: int = 0) -> dict:
    seeds = jax.random.split(jax.random.key(seed), 8)
    state = scatter_about(seeds[0], (E_TOTAL, 5, 512), 1.0, 6.0, ((0, 512),), jnp.float32)
    velocity = scatter_about(seeds[1], (E_TOTAL, 3), 1.0, 4.0, ((0, 512),), jnp.float32)
    interp_maps = scatter_about(seeds[2], (E_TOTAL, 3, 8, 8), 8 ** -0.5, 2.0, ((0, 512),), jnp.float32)
    neighbours = plant(jax.random.randint(seeds[3], (E_TOTAL, 6), 0, FACE_SLOTS), jax.random.fold_in(seeds[3], 1), 0, FACE_SLOTS - 1).astype(jnp.int32)
    send_faces = plant(jax.random.randint(seeds[4], (E_TOTAL,), 0, 6 * E_DEV), jax.random.fold_in(seeds[4], 1), 0, (6 * E_DEV) - 1).astype(jnp.int32)
    owner_device_keys = jax.random.split(jax.random.fold_in(seeds[5], 1), E_TOTAL // E_DEV)
    owner_device_turns = jax.random.permutation(jax.random.fold_in(seeds[5], 3), E_TOTAL // E_DEV)
    owner_device = jax.vmap(lambda own, number: deal_out(jax.random.fold_in(seeds[5], 2), own, number, E_DEV, N_AZ, 1, CAP, 1))(owner_device_keys, owner_device_turns).reshape((E_TOTAL, 1))
    owner_block = plant(jax.random.randint(seeds[6], (E_TOTAL,), 0, CB_DEV), jax.random.fold_in(seeds[6], 1), 0, CB_DEV - 1).astype(jnp.int32)
    return dict(state=state, velocity=velocity, interp_maps=interp_maps, neighbours=neighbours, send_faces=send_faces, owner_device=owner_device, owner_block=owner_block)


time_step = 0.02
penalty = 5.0
highest = lax.Precision.HIGHEST


def spectral_derivative():
    points = np.cos(np.pi * np.arange(8) / 7.0)
    ends = (np.arange(8) == 0) | (np.arange(8) == 7)
    scales = np.where(ends, 2.0, 1.0)
    signs = np.where(np.arange(8) % 2 == 0, 1.0, -1.0)
    differ = points[:, None] - points[None, :]
    offdiag = (scales[:, None] / scales[None, :]) * signs[:, None] * signs[None, :] / np.where(np.eye(8) > 0, 1.0, differ)
    inner = -points / (2.0 * np.where(ends, 1.0, 1.0 - points * points))
    corner = (2.0 * 49.0 + 1.0) / 6.0
    diagonal = np.where(np.arange(8) == 0, corner, np.where(np.arange(8) == 7, -corner, inner))
    return np.where(np.eye(8) > 0, diagonal[:, None], offdiag)


def derivative_table():
    deriv = spectral_derivative()
    along_x = np.kron(deriv, np.eye(64))
    along_y = np.kron(np.eye(8), np.kron(deriv, np.eye(8)))
    along_z = np.kron(np.eye(64), deriv)
    return np.concatenate([along_x.T, along_y.T, along_z.T], axis=1)


def face_selector():
    node_grid = np.arange(512).reshape(8, 8, 8)
    face_lists = [node_grid[0], node_grid[7], node_grid[:, 0], node_grid[:, 7], node_grid[:, :, 0], node_grid[:, :, 7]]
    picked = np.concatenate([square.reshape(-1) for square in face_lists])
    return (np.arange(512)[:, None] == picked[None, :]).astype(np.float32)


def group_rate(state, velocity, neighbours, send_faces):
    slices = velocity.shape[0]
    elements = velocity.shape[1]
    deriv = jnp.asarray(derivative_table(), jnp.float32)
    selector = jnp.asarray(face_selector(), jnp.float32)
    flat_state = state.reshape(slices * elements * 5, 512)
    derivs = jnp.dot(flat_state, deriv, precision=highest, preferred_element_type=jnp.float32)
    derivs = derivs.reshape(slices, elements, 5, 3, 512)
    advect = -jnp.einsum('sed,secdn->secn', velocity, derivs, precision=highest)
    own_faces = jnp.dot(flat_state, selector, precision=highest, preferred_element_type=jnp.float32)
    own_faces = own_faces.reshape(slices, elements, 5, 6, 64)
    local_table = own_faces.transpose(0, 1, 3, 2, 4).reshape(slices, elements * 6, 320)
    shared = jnp.take_along_axis(local_table, send_faces.astype(jnp.int32)[:, :, None], axis=1)
    gathered = shared.reshape(slices * elements, 320)
    tables = jnp.concatenate([local_table, jnp.broadcast_to(gathered[None], (slices, slices * elements, 320))], axis=1)
    lookup = neighbours.astype(jnp.int32).reshape(slices, elements * 6)[:, :, None]
    facing = jnp.take_along_axis(tables, lookup, axis=1)
    facing = facing.reshape(slices, elements, 6, 5, 64).transpose(0, 1, 3, 2, 4)
    face_jump = penalty * (facing - own_faces)
    lifted = jnp.dot(face_jump.reshape(-1, 384), selector.T, precision=highest, preferred_element_type=jnp.float32)
    return advect + lifted.reshape(slices, elements, 5, 512)


def interpolate(flat_state, interp_maps):
    node_cube = flat_state.reshape(-1, 5, 8, 8, 8)
    partial_value = jnp.einsum('erx,ecxyz->ecryz', interp_maps[:, 1], node_cube, precision=highest)
    partial_value = jnp.einsum('ety,ecryz->ectrz', interp_maps[:, 0], partial_value, precision=highest)
    partial_value = jnp.einsum('eqz,ectrz->ectrq', interp_maps[:, 2], partial_value, precision=highest)
    return partial_value.reshape(-1, 5 * 512)


def reference(state, velocity, interp_maps, neighbours, send_faces, owner_device, owner_block):
    grouped = (state.reshape(N_AZ, N_AX, E_DEV, 5, 512), velocity.reshape(N_AZ, N_AX, E_DEV, 3),
               neighbours.reshape(N_AZ, N_AX, E_DEV, 6), send_faces.reshape(N_AZ, N_AX, E_DEV),
               interp_maps.reshape(N_AZ, N_AX * E_DEV, 3, 8, 8))

    def advance(group_data):
        block_state, block_velocity, block_neighbours, block_sends, block_maps = group_data
        first_section = block_state + time_step * group_rate(block_state, block_velocity, block_neighbours, block_sends)
        second = 0.5 * (block_state + first_section + time_step * group_rate(first_section, block_velocity, block_neighbours, block_sends))
        return second, interpolate(second.reshape(-1, 5, 512), block_maps)

    advanced, blocks = lax.map(advance, grouped)
    slice_index = jnp.arange(N_AX, dtype=jnp.int32)[None, :, None]
    owners = owner_device.astype(jnp.int32).reshape(N_AZ, N_AX, E_DEV)
    targets = (owners * N_AX + slice_index) * CB_DEV + owner_block.astype(jnp.int32).reshape(N_AZ, N_AX, E_DEV)
    cylinder = jax.ops.segment_sum(blocks.reshape(-1, 2560), targets.reshape(-1), num_segments=N_AZ * N_AX * CB_DEV)
    cylinder = cylinder.reshape(N_AZ, N_AX, TB, PB, 5, 8, 64)
    cycle_data = cylinder.transpose(1, 4, 3, 6, 0, 2, 5).reshape(N_AX, 5, PB * 64, NTH)
    coeffs = jnp.fft.fft(cycle_data, axis=-1)
    stacked = jnp.stack([jnp.real(coeffs), jnp.imag(coeffs)]) * (NTH ** -0.5)
    stacked = stacked.reshape(2, N_AX, 5, N_AZ, CYCLE_DEV, NTH).transpose(0, 2, 3, 1, 4, 5)
    spectrum = stacked.reshape(2, 5, CYCLES, NTH)
    return advanced.reshape(E_TOTAL, 5, 512), spectrum
```

```python
import functools

import jax
import jax.numpy as jnp
import ml_dtypes
import numpy as np
from jax import lax
from jax.experimental import pallas as pl
from jax.experimental.pallas import tpu as pltpu
from jax.sharding import PartitionSpec as P

MESH = pl.DeviceIdType.MESH
F32 = jnp.float32
BF16 = jnp.bfloat16
E = 48
C = 5
ROWS = 6 * E
HALF = E // 2
STEP = 0.02
LIFT = 0.02 * 5.0


def spectral_derivative():
    points = np.cos(np.pi * np.arange(8) / 7.0)
    ends = (np.arange(8) == 0) | (np.arange(8) == 7)
    scales = np.where(ends, 2.0, 1.0)
    signs = np.where(np.arange(8) % 2 == 0, 1.0, -1.0)
    differ = points[:, None] - points[None, :]
    offdiag = (
        scales[:, None]
        / scales[None, :]
        * signs[:, None]
        * signs[None, :]
        / np.where(np.eye(8) > 0, 1.0, differ)
    )
    inner = -points / (2.0 * np.where(ends, 1.0, 1.0 - points * points))
    corner = (2.0 * 49.0 + 1.0) / 6.0
    diagonal = np.where(np.arange(8) == 0, corner, np.where(np.arange(8) == 7, -corner, inner))
    return np.where(np.eye(8) > 0, diagonal[:, None], offdiag)


DERIV = [[float(np.float32(v)) for v in row] for row in spectral_derivative()]


def dft_tables():
    tp, t2, j = np.meshgrid(np.arange(4), np.arange(2), np.arange(64), indexing="ij")
    theta = (8 * j + 2 * tp + t2).reshape(-1)
    phase = (theta[:, None] * np.arange(512)[None, :]) % 512
    angle = phase * (2.0 * np.pi / 512)
    table = np.concatenate([np.cos(angle), -np.sin(angle)], axis=1) * 512**-0.5
    high = table.astype(ml_dtypes.bfloat16)
    low = (table - high.astype(np.float64)).astype(ml_dtypes.bfloat16)
    return np.stack([high, low])


TABLES = dft_tables()


def contract(coef, tiles):
    total = coef(0) * tiles[0]
    for k in range(1, len(tiles)):
        total = total + coef(k) * tiles[k]
    return total


def kernel(
    n_ax,
    state_ref,
    vel_ref,
    maps_ref,
    owner_ref,
    block_ref,
    nbr_ref,
    send_ref,
    dft_ref,
    new_ref,
    spec_ref,
    flat,
    u,
    a,
    b,
    b2,
    vel,
    mt,
    fr,
    local,
    tab0,
    tab1,
    gat,
    wt,
    xs,
    xr,
    acc,
    zs,
    zr,
    dft,
    ag_send,
    up_recv,
    dn_recv,
    sib_recv,
    x_send,
    x_recv,
    z_send,
    z_recv,
    dft_sem,
):
    az, ax = lax.axis_index("az"), lax.axis_index("ax")
    z, x = az // 4, az % 4
    up, dn = lax.rem(ax + 2, n_ax), lax.rem(ax + n_ax - 2, n_ax)
    sib = ax + 1 - 2 * lax.rem(ax, 2)

    tabs = (tab0, tab1)
    barrier = pltpu.get_barrier_semaphore()
    for peer in (up, dn, sib):
        pl.semaphore_signal(barrier, inc=1, device_id=(az, peer), device_id_type=MESH)
    for d in range(1, 4):
        pl.semaphore_signal(
            barrier, inc=1, device_id=(z * 4 + lax.rem(x + d, 4), ax), device_id_type=MESH
        )
    for d in range(1, 8):
        pl.semaphore_signal(
            barrier, inc=1, device_id=(lax.rem(z + d, 8) * 4 + x, ax), device_id_type=MESH
        )

    dft_copy = pltpu.make_async_copy(dft_ref, dft, dft_sem)
    dft_copy.start()

    lane = lax.broadcasted_iota(jnp.int32, (8, 128), 1)

    def low_half(rows):
        return lax.broadcasted_iota(jnp.int32, (rows, 128), 1) < 64

    flat[0:240] = state_ref[...]
    flat[240:256] = jnp.zeros((16, 512), F32)
    for h in range(2):
        for n in range(4):
            u[h, 128 * n : 128 * n + 128, :] = flat[
                128 * h : 128 * h + 128, 128 * n : 128 * n + 128
            ].T

    def face_pair(ref, h, pair):
        if pair == 0:
            return jnp.concatenate([ref[h, 0:64, :], ref[h, 448:512, :]], axis=0)
        if pair == 1:
            return jnp.concatenate(
                [ref[h, 64 * i + o : 64 * i + o + 8, :] for o in (0, 56) for i in range(8)], axis=0
            )
        return jnp.concatenate(
            [ref[h, pl.ds(0, 64, stride=8), :], ref[h, pl.ds(7, 64, stride=8), :]], axis=0
        )

    def publish(ref, g):
        for pair in range(3):
            for h in range(2):
                fr[pair, 128 * h : 128 * h + 128, :] = face_pair(ref, h, pair).T
        for pair in range(3):
            for p in range(3):
                first = fr[pair, 96 * p : 96 * p + 48, :]
                if p < 2:
                    second = fr[pair, 96 * p + 48 : 96 * p + 96, :]
                else:
                    second = jnp.zeros((48, 128), F32)
                low = low_half(48)
                even = jnp.where(low, first, pltpu.roll(second, 64, 1))
                odd = jnp.where(low, pltpu.roll(first, 64, 1), second)
                for table in (local, tabs[g]):
                    table[p, pl.ds(2 * pair, 48, stride=6), :] = even
                    table[p, pl.ds(2 * pair + 1, 48, stride=6), :] = odd
        own = pl.multiple_of(ROWS + E * ax, 8)

        @pl.loop(0, 12)
        def _(i):
            for k in range(4):
                s = 4 * i + k
                tabs[g][:, pl.ds(own + s, 1), :] = local[:, pl.ds(send_ref[0, s], 1), :]

    def ag_copy(g, source, ch, target, send, recv):
        rows = pl.ds(pl.multiple_of(ROWS + E * source + HALF * ch, 8), HALF)
        return pltpu.make_async_remote_copy(
            src_ref=tabs[g].at[:, rows, :],
            dst_ref=tabs[g].at[:, rows, :],
            send_sem=send,
            recv_sem=recv,
            device_id=(az, target),
            device_id_type=MESH,
        )

    def below(base, h):
        return lax.rem(base + n_ax - 2 * h, n_ax)

    def above(base, h):
        return lax.rem(base + 2 * h, n_ax)

    arrivals = [
        (h, ch, rising)
        for h in range(1, 5)
        for ch in range(2)
        for rising in (True, False)
        if h < 4 or (ch == 0) == rising
    ]

    class Gather:
        def __init__(self, g):
            self.g = g
            self.sent = []

        def send(self, source, ch, target, recv):
            copy = ag_copy(self.g, source, ch, target, ag_send.at[self.g, len(self.sent)], recv)
            copy.start()
            self.sent.append(copy)

        def start(self):
            g = self.g
            for ch in range(2):
                self.send(ax, ch, up, up_recv.at[g, 0, ch])
                self.send(ax, ch, dn, dn_recv.at[g, 0, ch])
            for ch in range(2):
                self.send(ax, ch, sib, sib_recv.at[g, ch])

        def hop(self, hops):
            g = self.g
            for k, (h, ch, rising) in enumerate(arrivals):
                if h != hops:
                    continue
                source = below(ax, h) if rising else above(ax, h)
                sems = up_recv if rising else dn_recv
                target = up if rising else dn
                ag_copy(
                    g, source, ch, target, ag_send.at[g, 0], sems.at[g, h - 1, ch]
                ).wait_recv()
                if h < 3 or (h == 3 and (ch == 0) == rising):
                    self.send(source, ch, target, sems.at[g, h, ch])
                self.send(source, ch, sib, sib_recv.at[g, 2 + k])

        def finish(self):
            g = self.g
            for ch in range(2):
                ag_copy(g, sib, ch, sib, ag_send.at[g, 0], sib_recv.at[g, ch]).wait_recv()
            for k, (h, ch, rising) in enumerate(arrivals):
                source = below(sib, h) if rising else above(sib, h)
                ag_copy(g, source, ch, sib, ag_send.at[g, 0], sib_recv.at[g, 2 + k]).wait_recv()

        def drain(self):
            for copy in self.sent:
                copy.wait_send()

    def along_x(src, dst):
        @pl.loop(0, 8)
        def _(y):
            for h in range(2):
                rows = [pl.ds(pl.multiple_of(64 * i + 8 * y, 8), 8) for i in range(8)]
                tiles = [src[h, rows[i], :] for i in range(8)]
                v = vel[0, h]
                for i in range(8):
                    dst[h, rows[i], :] = tiles[i] + v * contract(lambda k: DERIV[i][k], tiles)

    def along_yz(src, dst):
        @pl.loop(0, 8)
        def _(i):
            for h in range(2):
                rows = [pl.ds(pl.multiple_of(64 * i + 8 * y, 8), 8) for y in range(8)]
                tiles = [src[h, rows[y], :] for y in range(8)]
                v = vel[1, h]
                for y in range(8):
                    dst[h, rows[y], :] += v * contract(lambda k: DERIV[y][k], tiles)
                cols = [pl.ds(64 * i + q, 8, stride=8) for q in range(8)]
                tiles = [src[h, cols[q], :] for q in range(8)]
                v = vel[2, h]
                for q in range(8):
                    dst[h, cols[q], :] += v * contract(lambda k: DERIV[q][k], tiles)

    def lift(dst, value, scale):
        for h in range(2):
            dst[h, 0:64, :] += scale * value(h, 0)
            dst[h, 448:512, :] += scale * value(h, 1)
            for f, o in ((2, 0), (3, 56)):
                rows = scale * value(h, f)
                for i in range(8):
                    dst[h, 64 * i + o : 64 * i + o + 8, :] += rows[8 * i : 8 * i + 8]
            dst[h, pl.ds(0, 64, stride=8), :] += scale * value(h, 4)
            dst[h, pl.ds(7, 64, stride=8), :] += scale * value(h, 5)

    def own_face(ref):
        def value(h, f):
            pair = face_pair(ref, h, f // 2)
            return pair[64 * (f % 2) : 64 * (f % 2) + 64]

        return value

    def facing(g):
        @pl.loop(0, E)
        def _(e):
            for f in range(6):
                gat[:, pl.ds(f * E + e, 1), :] = tabs[g][:, pl.ds(nbr_ref[f, e], 1), :]

        for pair in range(3):
            for c in range(C):
                first = gat[c // 2, 96 * pair : 96 * pair + 48, :]
                second = gat[c // 2, 96 * pair + 48 : 96 * pair + 96, :]
                low = low_half(48)
                if c % 2 == 0:
                    both = jnp.where(low, first, pltpu.roll(second, 64, 1))
                else:
                    both = jnp.where(low, pltpu.roll(first, 64, 1), second)
                fr[pair, 48 * c : 48 * c + 48, :] = both
            for h in range(2):
                wt[h, 128 * pair : 128 * pair + 128, :] = fr[
                    pair, 128 * h : 128 * h + 128, :
                ].T

    def from_wt(h, f):
        return wt[h, 64 * f : 64 * f + 64, :]

    publish(u, 0)
    pl.semaphore_wait(barrier, 13)
    gather = Gather(0)
    gather.start()

    spread = (
        lax.rem(lax.broadcasted_iota(jnp.int32, (E, 256), 1), E)
        == lax.broadcasted_iota(jnp.int32, (E, 256), 0)
    ) & (lax.broadcasted_iota(jnp.int32, (E, 256), 1) < C * E)
    spread = spread.astype(F32)

    def over_lanes(rows):
        return jnp.dot(rows, spread, precision=lax.Precision.HIGHEST, preferred_element_type=F32)

    speeds = over_lanes(-STEP * vel_ref[...])
    maps = over_lanes(maps_ref[...])
    block = block_ref[...]
    label = lax.rem(block, 4) * 64 + owner_ref[...] * 2 + block // 4
    labels = over_lanes(label.astype(F32))
    for h in range(2):
        for d in range(3):
            vel[d, h] = jnp.broadcast_to(speeds[d : d + 1, 128 * h : 128 * h + 128], (8, 128))
        mt[h] = maps[:, 128 * h : 128 * h + 128]
        for d in range(4):
            xs[d, h, 128:136, :] = jnp.broadcast_to(
                labels[:, 128 * h : 128 * h + 128], (8, 128)
            )

    fr[:, 240:256, :] = jnp.zeros((3, 16, 128), F32)
    along_x(u, a)
    gather.hop(1)
    along_yz(u, a)
    gather.hop(2)
    lift(a, own_face(u), -LIFT)
    gather.hop(3)
    gather.hop(4)
    gather.finish()
    facing(0)
    lift(a, from_wt, LIFT)

    publish(a, 1)
    gather2 = Gather(1)
    gather2.start()
    along_x(a, b)
    gather2.hop(1)
    along_yz(a, b)
    gather2.hop(2)
    lift(b, own_face(a), -LIFT)
    b[...] = 0.5 * (u[...] + b[...])
    gather2.hop(3)
    gather2.hop(4)
    gather2.finish()
    facing(1)
    lift(b, from_wt, 0.5 * LIFT)

    def coef(h, which, out):
        return lambda k: mt[h, pl.ds(64 * which + 8 * out + k, 1), :]

    @pl.loop(0, 8)
    def _(y):
        for h in range(2):
            rows = [pl.ds(pl.multiple_of(64 * i + 8 * y, 8), 8) for i in range(8)]
            tiles = [b[h, rows[i], :] for i in range(8)]
            for r in range(8):
                b2[h, rows[r], :] = contract(coef(h, 1, r), tiles)

    @pl.loop(0, 8)
    def _(r):
        for h in range(2):
            rows = [pl.ds(pl.multiple_of(64 * r + 8 * i, 8), 8) for i in range(8)]
            tiles = [b2[h, rows[i], :] for i in range(8)]
            for t in range(8):
                a[h, rows[t], :] = contract(coef(h, 0, t), tiles)
            tiles = [a[h, pl.ds(64 * r + q, 8, stride=8), :] for q in range(8)]
            for q in range(8):
                xs[r % 4, h, pl.ds((r // 4) * 64 + q, 8, stride=8), :] = contract(
                    coef(h, 2, q), tiles
                )

    x_copies = []
    for d in (1, 3, 2):
        target = lax.rem(x + d, 4)
        copy = pltpu.make_async_remote_copy(
            src_ref=xs.at[target],
            dst_ref=xr.at[d - 1],
            send_sem=x_send.at[d - 1],
            recv_sem=x_recv.at[d - 1],
            device_id=(z * 4 + target, ax),
            device_id_type=MESH,
        )
        copy.start()
        x_copies.append(copy)

    for h in range(2):
        for n in range(4):
            flat[128 * h : 128 * h + 128, 128 * n : 128 * n + 128] = b[
                h, 128 * n : 128 * n + 128, :
            ].T
    new_ref[...] = flat[0:240]

    wide = lax.broadcasted_iota(jnp.int32, (128, 256), 1)

    def collect(ref, first):
        values = jnp.concatenate([ref[0, 0:128, :], ref[1, 0:128, :]], axis=1)
        names = jnp.concatenate([ref[0, 128:129, :], ref[1, 128:129, :]], axis=1)
        place = (
            lax.broadcasted_iota(jnp.int32, (256, 256), 0) == names.astype(jnp.int32)
        ).astype(BF16)
        high = values.astype(BF16).astype(F32)
        low = values - high
        for c in range(C):
            mine = (wide >= E * c) & (wide < E * c + E)
            part = 0.0
            for term in (high, low):
                part = part + lax.dot_general(
                    jnp.where(mine, term, 0.0).astype(BF16),
                    place,
                    (((1,), (1,)), ((), ())),
                    preferred_element_type=F32,
                )
            if first:
                acc[c] = part
            else:
                acc[c] += part

    collect(xs.at[x], True)
    for copy, d in zip(x_copies, (1, 3, 2)):
        copy.wait_recv()
        collect(xr.at[d - 1], False)

    low8 = lane < 64
    for c in range(C):
        for r2 in range(2):
            for tp in range(4):
                o = 64 * r2 + 16 * tp
                for v in range(2):
                    even = acc[c, o : o + 8, 128 * v : 128 * v + 128]
                    odd = acc[c, o + 8 : o + 16, 128 * v : 128 * v + 128]
                    zs[4 * v + r2, c, tp] = jnp.where(low8, even, pltpu.roll(odd, 64, 1))
                    zs[4 * v + 2 + r2, c, tp] = jnp.where(low8, pltpu.roll(even, 64, 1), odd)

    z_copies = []
    for d in (4, 3, 5, 2, 6, 1, 7):
        target = lax.rem(z + d, 8)
        copy = pltpu.make_async_remote_copy(
            src_ref=zs.at[target],
            dst_ref=zr.at[d - 1],
            send_sem=z_send.at[d - 1],
            recv_sem=z_recv.at[d - 1],
            device_id=(target * 4 + x, ax),
            device_id_type=MESH,
        )
        copy.start()
        z_copies.append(copy)

    total = zs[z]
    for copy, d in reversed(list(zip(z_copies, (4, 3, 5, 2, 6, 1, 7)))):
        copy.wait_recv()
        total = total + zr[d - 1]

    dft_copy.wait()
    series = jnp.concatenate([total[:, tp].reshape(8 * C, 128) for tp in range(4)], axis=1)
    high = series.astype(BF16)
    low = (series - high.astype(F32)).astype(BF16)
    for half in range(2):
        cols = pl.ds(512 * half, 512)
        spec_ref[half] = (
            jnp.dot(high, dft[0, :, cols], preferred_element_type=F32)
            + jnp.dot(low, dft[0, :, cols], preferred_element_type=F32)
            + jnp.dot(high, dft[1, :, cols], preferred_element_type=F32)
        )

    gather.drain()
    gather2.drain()
    for copy in x_copies + z_copies:
        copy.wait_send()


def per_device(n_ax, state, velocity, interp_maps, neighbours, send_faces, owner_device, owner_block):
    vmem = pl.BlockSpec(memory_space=pltpu.VMEM)
    smem = pl.BlockSpec(memory_space=pltpu.SMEM)
    dma = pltpu.SemaphoreType.DMA
    half_nodes = pltpu.VMEM((2, 512, 128), F32)
    new, spec = pl.pallas_call(
        functools.partial(kernel, n_ax),
        out_shape=(
            jax.ShapeDtypeStruct((C * E, 512), F32),
            jax.ShapeDtypeStruct((2, 8 * C, 512), F32),
        ),
        in_specs=[vmem] * 5 + [smem] * 2 + [pl.BlockSpec(memory_space=pl.ANY)],
        out_specs=(vmem, vmem),
        scratch_shapes=[
            pltpu.VMEM((256, 512), F32),
            half_nodes,
            half_nodes,
            half_nodes,
            half_nodes,
            pltpu.VMEM((3, 2, 8, 128), F32),
            pltpu.VMEM((2, 192, 128), F32),
            pltpu.VMEM((3, 256, 128), F32),
            pltpu.VMEM((3, ROWS, 128), F32),
            pltpu.VMEM((3, ROWS + E * n_ax, 128), F32),
            pltpu.VMEM((3, ROWS + E * n_ax, 128), F32),
            pltpu.VMEM((3, ROWS, 128), F32),
            pltpu.VMEM((2, 384, 128), F32),
            pltpu.VMEM((4, 2, 136, 128), F32),
            pltpu.VMEM((3, 2, 136, 128), F32),
            pltpu.VMEM((C, 128, 256), F32),
            pltpu.VMEM((8, C, 4, 8, 128), F32),
            pltpu.VMEM((7, C, 4, 8, 128), F32),
            pltpu.VMEM((2, 512, 1024), BF16),
            dma((2, 30)),
            dma((2, 4, 2)),
            dma((2, 4, 2)),
            dma((2, 16)),
            dma((3,)),
            dma((3,)),
            dma((7,)),
            dma((7,)),
            dma,
        ],
        compiler_params=pltpu.CompilerParams(
            collective_id=0, has_side_effects=True, vmem_limit_bytes=56 * 1024 * 1024
        ),
        name="advance",
    )(
        state.transpose(1, 0, 2).reshape(C * E, 512),
        velocity.T,
        interp_maps.transpose(1, 2, 3, 0).reshape(192, E),
        owner_device.reshape(1, E),
        owner_block.reshape(1, E),
        neighbours.T,
        send_faces.reshape(1, E),
        jnp.asarray(TABLES),
    )
    return (
        new.reshape(C, E, 512).transpose(1, 0, 2),
        spec.reshape(2, C, 8, 512),
    )


def solution(mesh):
    return jax.shard_map(
        functools.partial(per_device, mesh.shape["ax"]),
        mesh=mesh,
        in_specs=(
            P(("az", "ax"), None, None),
            P(("az", "ax"), None),
            P(("az", "ax"), None, None, None),
            P(("az", "ax"), None),
            P(("az", "ax")),
            P(("az", "ax"), None),
            P(("az", "ax")),
        ),
        out_specs=(P(("az", "ax"), None, None), P(None, None, ("az", "ax"), None)),
        check_vma=False,
    )
```

```python
import functools

import jax
import jax.numpy as jnp
import ml_dtypes
import numpy as np
from jax import lax
from jax.experimental import pallas as pl
from jax.experimental.pallas import tpu as pltpu
from jax.sharding import PartitionSpec as P

MESH = pl.DeviceIdType.MESH
F32 = jnp.float32
BF16 = jnp.bfloat16
E = 48
C = 5
ROWS = 6 * E
CHAINED = ()
Z_STEPS = 5 * len(CHAINED) + 2 * (4 - len(CHAINED))
Z_ENDS = 2 * len(CHAINED) + 4 * (4 - len(CHAINED))
BLOCK = 120
PIECES = ((0, 64), (64, 56))
STEP = 0.02
LIFT = 0.02 * 5.0


def spectral_derivative():
    points = np.cos(np.pi * np.arange(8) / 7.0)
    ends = (np.arange(8) == 0) | (np.arange(8) == 7)
    scales = np.where(ends, 2.0, 1.0)
    signs = np.where(np.arange(8) % 2 == 0, 1.0, -1.0)
    differ = points[:, None] - points[None, :]
    offdiag = (
        scales[:, None]
        / scales[None, :]
        * signs[:, None]
        * signs[None, :]
        / np.where(np.eye(8) > 0, 1.0, differ)
    )
    inner = -points / (2.0 * np.where(ends, 1.0, 1.0 - points * points))
    corner = (2.0 * 49.0 + 1.0) / 6.0
    diagonal = np.where(np.arange(8) == 0, corner, np.where(np.arange(8) == 7, -corner, inner))
    return np.where(np.eye(8) > 0, diagonal[:, None], offdiag)


DERIV = [[float(np.float32(v)) for v in row] for row in spectral_derivative()]


def dft_tables():
    j, m0 = np.meshgrid(np.arange(64), np.arange(64), indexing="ij")
    angle = (j * m0 % 64) * (2.0 * np.pi / 64)
    points = np.concatenate([np.cos(angle)] * 2 + [-np.sin(angle)] * 2, axis=1)
    table = np.zeros((2, 64, 2, 256))
    table[0, :, 0], table[1, :, 1] = points, points
    table = table.reshape(128, 512)
    high = table.astype(ml_dtypes.bfloat16)
    low = (table - high.astype(np.float64)).astype(ml_dtypes.bfloat16)
    t, m = np.meshgrid(np.arange(8), np.arange(512), indexing="ij")
    angle = (t * m % 512) * (2.0 * np.pi / 512)
    twiddle = np.stack([np.cos(angle), -np.sin(angle)]) * 512**-0.5
    return np.stack([high, low]), twiddle.astype(np.float32)


TABLES, TWIDDLE = dft_tables()


def contract(coef, tiles):
    total = coef(0) * tiles[0]
    for k in range(1, len(tiles)):
        total = total + coef(k) * tiles[k]
    return total


def kernel(
    n_ax,
    vel_hbm,
    maps_hbm,
    owner_hbm,
    block_hbm,
    nbv_hbm,
    send_hbm,
    state_ref,
    new_ref,
    sum_hbm,
    sum_ref,
    flat,
    u,
    a,
    b,
    b2,
    vel,
    mt,
    fr,
    local,
    last,
    tab0,
    tab1,
    gat,
    where_v,
    where,
    upper,
    vel_ref,
    maps_ref,
    owner_ref,
    block_ref,
    nbv_ref,
    send_ref,
    in_sem,
    where_sem,
    wt,
    names,
    names_in,
    place,
    xs,
    xr,
    zs,
    zr,
    state_sem,
    new_sem,
    ag_send,
    y_recv,
    sib_recv,
    name_send,
    name_recv,
    x_send,
    x_recv,
    z_send,
    z_recv,
    z_last,
):
    az, ax = lax.axis_index("az"), lax.axis_index("ax")
    z, x = az // 4, az % 4
    up, dn = lax.rem(ax + 2, n_ax), lax.rem(ax + n_ax - 2, n_ax)
    up2, dn2 = lax.rem(ax + 4, n_ax), lax.rem(ax + n_ax - 4, n_ax)
    sib = ax + 1 - 2 * lax.rem(ax, 2)
    far = BLOCK * n_ax

    tabs = (tab0, tab1)
    state_copies = [
        pltpu.make_async_copy(state_ref.at[:, part], flat.at[0:240, part], state_sem.at[n])
        for n, part in enumerate((pl.ds(0, 256), pl.ds(256, 256)))
    ]
    operand_copies = [
        pltpu.make_async_copy(src, dst, in_sem.at[n])
        for n, (src, dst) in enumerate(
            (
                (send_hbm, send_ref),
                (vel_hbm, vel_ref),
                (owner_hbm, owner_ref),
                (block_hbm, block_ref),
                (nbv_hbm, nbv_ref),
                (maps_hbm, maps_ref),
            )
        )
    ]
    for copy in state_copies + operand_copies:
        copy.start()
    barrier = pltpu.get_barrier_semaphore()
    for peer in (up, dn, up2, dn2, sib):
        pl.semaphore_signal(barrier, inc=1, device_id=(az, peer), device_id_type=MESH)
    for d in range(1, 4):
        pl.semaphore_signal(
            barrier, inc=1, device_id=(z * 4 + lax.rem(x + d, 4), ax), device_id_type=MESH
        )
    for d in (1, 2, 6, 7):
        pl.semaphore_signal(
            barrier, inc=1, device_id=(lax.rem(z + d, 8) * 4 + x, ax), device_id_type=MESH
        )

    lane = lax.broadcasted_iota(jnp.int32, (8, 128), 1)

    def low_half(rows):
        return lax.broadcasted_iota(jnp.int32, (rows, 128), 1) < 64

    flat[240:256] = jnp.zeros((16, 512), F32)
    for n in range(4):
        if n % 2 == 0:
            state_copies[n // 2].wait()
        for h in range(2):
            u[h, 128 * n : 128 * n + 128, :] = flat[
                128 * h : 128 * h + 128, 128 * n : 128 * n + 128
            ].T
    for copy in operand_copies:
        copy.wait()

    def face_pair(ref, h, pair):
        if pair == 0:
            return jnp.concatenate([ref[h, 0:64, :], ref[h, 448:512, :]], axis=0)
        if pair == 1:
            return jnp.concatenate(
                [ref[h, 64 * i + o : 64 * i + o + 8, :] for o in (0, 56) for i in range(8)], axis=0
            )
        return jnp.concatenate(
            [ref[h, pl.ds(0, 64, stride=8), :], ref[h, pl.ds(7, 64, stride=8), :]], axis=0
        )

    def publish(ref, g):
        for pair in range(3):
            for h in range(2):
                fr[pair, 128 * h : 128 * h + 128, :] = face_pair(ref, h, pair).T
        for pair in range(3):
            for p in range(3):
                first = fr[pair, 96 * p : 96 * p + 48, :]
                if p < 2:
                    second = fr[pair, 96 * p + 48 : 96 * p + 96, :]
                else:
                    second = jnp.zeros((48, 128), F32)
                low = low_half(48)
                even = jnp.where(low, first, pltpu.roll(second, 64, 1))
                odd = jnp.where(low, pltpu.roll(first, 64, 1), second)
                table = tabs[g]
                for o, rows in ((0, even), (1, odd)):
                    f = 2 * pair + o
                    local[p, pl.ds(f, 48, stride=6), :] = rows
                    if p < 2:
                        for k in range(6):
                            table[pl.ds(far + 96 * k + 48 * p + f, 8, stride=6), :] = rows[
                                8 * k : 8 * k + 8
                            ]
                    else:
                        table[pl.ds(far + 2 * ROWS + f, 48, stride=6), :] = rows
        own = pl.multiple_of(BLOCK * ax, 8)
        table = tabs[g]

        @pl.loop(0, 12)
        def _(i):
            for k in range(4):
                s = 4 * i + k
                row = send_ref[0, s]
                for p in range(2):
                    table[pl.ds(own + 48 * p + s, 1), :] = local[p, pl.ds(row, 1), :]
                last[pl.ds(s, 1), :] = local[2, pl.ds(row, 1), :]

        table[pl.ds(own + 96, 24), :] = jnp.where(
            low_half(24), last[0:24, :], pltpu.roll(last[24:48, :], 64, 1)
        )

    def ag_copy(g, source, piece, target, send, recv):
        start, count = PIECES[piece]
        rows = pl.ds(pl.multiple_of(BLOCK * source + start, 8), count)
        return pltpu.make_async_remote_copy(
            src_ref=tabs[g].at[rows, :],
            dst_ref=tabs[g].at[rows, :],
            send_sem=send,
            recv_sem=recv,
            device_id=(az, target),
            device_id_type=MESH,
        )

    def behind(way, h):
        return lax.rem(ax + (n_ax - 2 * h if way == 0 else 2 * h), n_ax)

    class Gather:
        ways = ((0, up, up2), (1, dn, dn2))

        def __init__(self, g):
            self.g = g
            self.sent = 0

        def send(self, source, piece, target, recv):
            ag_copy(self.g, source, piece, target, ag_send.at[self.g], recv).start()
            self.sent += PIECES[piece][1]

        def share(self, source, piece):
            self.send(source, piece, sib, sib_recv.at[self.g])

        def start(self):
            g = self.g
            for h in (1, 0):
                for k in range(2):
                    for way, *targets in self.ways:
                        piece = 1 - k if way else k
                        self.send(ax, piece, targets[h], y_recv.at[g, way, h, piece])
            for piece in range(2):
                self.share(ax, piece)

        def hop(self, h):
            g = self.g
            for k in range(2 if h < 4 else 1):
                for way, one, two in self.ways:
                    piece = 1 - k if way else k
                    source = behind(way, h)
                    ag_copy(
                        g, source, piece, one, ag_send.at[g], y_recv.at[g, way, h - 1, piece]
                    ).wait_recv()
                    if h == 2:
                        if k == 0:
                            self.send(source, piece, two, y_recv.at[g, way, 3, piece])
                        self.send(source, piece, one, y_recv.at[g, way, 2, piece])
                    self.share(source, piece)

        def whole(self, count):
            rows = pl.ds(0, count)
            return pltpu.make_async_remote_copy(
                src_ref=tabs[self.g].at[rows, :],
                dst_ref=tabs[self.g].at[rows, :],
                send_sem=ag_send.at[self.g],
                recv_sem=sib_recv.at[self.g],
                device_id=(az, sib),
                device_id_type=MESH,
            )

        def finish(self):
            self.whole(8 * BLOCK).wait_recv()

        def drain(self):
            self.whole(self.sent).wait_send()

    def along_x(src, dst):
        @pl.loop(0, 8)
        def _(y):
            for h in range(2):
                rows = [pl.ds(pl.multiple_of(64 * i + 8 * y, 8), 8) for i in range(8)]
                tiles = [src[h, rows[i], :] for i in range(8)]
                v = vel[0, h]
                for i in range(8):
                    dst[h, rows[i], :] = tiles[i] + v * contract(lambda k: DERIV[i][k], tiles)

    def along_yz(src, dst):
        @pl.loop(0, 8)
        def _(i):
            for h in range(2):
                rows = [pl.ds(pl.multiple_of(64 * i + 8 * y, 8), 8) for y in range(8)]
                tiles = [src[h, rows[y], :] for y in range(8)]
                v = vel[1, h]
                for y in range(8):
                    dst[h, rows[y], :] += v * contract(lambda k: DERIV[y][k], tiles)
                cols = [pl.ds(64 * i + q, 8, stride=8) for q in range(8)]
                tiles = [src[h, cols[q], :] for q in range(8)]
                v = vel[2, h]
                for q in range(8):
                    dst[h, cols[q], :] += v * contract(lambda k: DERIV[q][k], tiles)

    def lift(dst, value, scale):
        for h in range(2):
            dst[h, 0:64, :] += scale * value(h, 0)
            dst[h, 448:512, :] += scale * value(h, 1)
            for f, o in ((2, 0), (3, 56)):
                rows = scale * value(h, f)
                for i in range(8):
                    dst[h, 64 * i + o : 64 * i + o + 8, :] += rows[8 * i : 8 * i + 8]
            dst[h, pl.ds(0, 64, stride=8), :] += scale * value(h, 4)
            dst[h, pl.ds(7, 64, stride=8), :] += scale * value(h, 5)

    def own_face(ref):
        def value(h, f):
            pair = face_pair(ref, h, f // 2)
            return pair[64 * (f % 2) : 64 * (f % 2) + 64]

        return value

    def facing(g):
        size = far + 3 * ROWS - 48
        views = (tabs[g].at[pl.ds(0, size), :], tabs[g].at[pl.ds(48, size), :], tabs[g])

        @pl.loop(0, E)
        def _(e):
            for f in range(6):
                pair, single = where[f, e], where[8 + f, e]
                for p, row in enumerate((pair, pair, single)):
                    gat[p, pl.ds(f * E + e, 1), :] = views[p][pl.ds(row, 1), :]


        def got(p, f):
            rows = gat[p, f * E : f * E + E, :]
            if p < 2:
                return rows
            return jnp.where(upper[f * E : f * E + E, :] > 0.5, pltpu.roll(rows, 64, 1), rows)

        low = low_half(48)
        for pair in range(3):
            for p in range(3):
                first, second = got(p, 2 * pair), got(p, 2 * pair + 1)
                fr[pair, 96 * p : 96 * p + 48, :] = jnp.where(
                    low, first, pltpu.roll(second, 64, 1)
                )
                if p < 2:
                    fr[pair, 96 * p + 48 : 96 * p + 96, :] = jnp.where(
                        low, pltpu.roll(first, 64, 1), second
                    )
            for h in range(2):
                wt[h, 128 * pair : 128 * pair + 128, :] = fr[
                    pair, 128 * h : 128 * h + 128, :
                ].T

    def from_wt(h, f):
        return wt[h, 64 * f : 64 * f + 64, :]

    def moved(ref, send, recv):
        return pltpu.make_async_remote_copy(
            src_ref=ref,
            dst_ref=ref,
            send_sem=send,
            recv_sem=recv,
            device_id=(az, sib),
            device_id_type=MESH,
        )

    publish(u, 0)
    pl.semaphore_wait(barrier, 12)
    gather = Gather(0)
    gather.start()

    spread = (
        lax.rem(lax.broadcasted_iota(jnp.int32, (E, 256), 1), E)
        == lax.broadcasted_iota(jnp.int32, (E, 256), 0)
    ) & (lax.broadcasted_iota(jnp.int32, (E, 256), 1) < C * E)
    spread = spread.astype(F32)

    def over_lanes(rows):
        return jnp.dot(rows, spread, precision=lax.Precision.HIGHEST, preferred_element_type=F32)

    speeds = over_lanes(-STEP * vel_ref[...])
    block = block_ref[...]
    label = lax.rem(block, 4) * 64 + owner_ref[...] * 2 + block // 4
    labels = over_lanes(label.astype(F32))
    for h in range(2):
        names[h] = jnp.broadcast_to(labels[:, 128 * h : 128 * h + 128], (8, 128))
        for d in range(3):
            vel[d, h] = jnp.broadcast_to(speeds[d : d + 1, 128 * h : 128 * h + 128], (8, 128))
    for d in range(1, 4):
        pltpu.make_async_remote_copy(
            src_ref=names,
            dst_ref=names_in.at[d - 1],
            send_sem=name_send,
            recv_sem=name_recv,
            device_id=(z * 4 + lax.rem(x + d, 4), ax),
            device_id_type=MESH,
        ).start()
    fr[:, 240:256, :] = jnp.zeros((3, 16, 128), F32)

    along_x(u, a)
    along_yz(u, a)
    lift(a, own_face(u), -LIFT)

    row = nbv_ref[...]
    inside = row < ROWS
    slot = row - ROWS
    device = slot // E
    slot = slot - E * device
    start = BLOCK * device
    upper_row = (~inside) & (slot >= 24)
    where_v[0:6, 0:E] = jnp.where(inside, far + row + 48 * (row // E), start + slot)
    where_v[8:14, 0:E] = jnp.where(
        inside, far + 2 * ROWS + row, start + 96 + slot - jnp.where(upper_row, 24, 0)
    )
    where_copy = pltpu.make_async_copy(where_v, where, where_sem)
    where_copy.start()
    folds = upper_row.astype(F32)
    diagonal = lax.broadcasted_iota(jnp.int32, (E, E), 0) == lax.broadcasted_iota(
        jnp.int32, (E, E), 1
    )
    for f in range(6):
        upper[f * E : f * E + E, :] = jnp.dot(
            jnp.where(diagonal, folds[f : f + 1, :], 0.0),
            jnp.ones((E, 128), F32),
            preferred_element_type=F32,
        )
    where_copy.wait()
    for h in (2, 1, 3, 4):
        gather.hop(h)
    gather.finish()
    facing(0)
    lift(a, from_wt, LIFT)

    publish(a, 1)
    gather2 = Gather(1)
    gather2.start()
    along_x(a, b)
    along_yz(a, b)
    lift(b, own_face(a), -LIFT)
    b[...] = 0.5 * (u[...] + b[...])
    maps = over_lanes(maps_ref[...])
    for h in range(2):
        mt[h] = maps[:, 128 * h : 128 * h + 128]

    def set_place(s, ref):
        label = jnp.concatenate([ref[0, 0:1, :], ref[1, 0:1, :]], axis=1).astype(jnp.int32)
        rows = lax.broadcasted_iota(jnp.int32, (256, 256), 0)
        place[s] = (rows == label).astype(F32).astype(BF16)

    set_place(0, names)
    moved(names_in, name_send, name_recv).wait_recv()
    for d in range(1, 4):
        set_place(d, names_in.at[d - 1])
    gather2.hop(2)
    gather2.hop(1)
    gather2.hop(3)
    gather2.hop(4)
    gather2.finish()
    facing(1)
    lift(b, from_wt, 0.5 * LIFT)

    def coef(h, which, out):
        return lambda k: mt[h, pl.ds(64 * which + 8 * out + k, 1), :]

    @pl.loop(0, 8)
    def _(y):
        for h in range(2):
            rows = [pl.ds(pl.multiple_of(64 * i + 8 * y, 8), 8) for i in range(8)]
            tiles = [b[h, rows[i], :] for i in range(8)]
            for r in range(8):
                b2[h, rows[r], :] = contract(coef(h, 1, r), tiles)

    @pl.loop(0, 8)
    def _(r):
        for h in range(2):
            tiles = [b2[h, pl.ds(64 * r + q, 8, stride=8), :] for q in range(8)]
            for q in range(8):
                a[h, pl.ds(64 * r + q, 8, stride=8), :] = contract(coef(h, 2, q), tiles)

    def sample(tp):
        @pl.loop(0, 8)
        def _(r):
            for h in range(2):
                rows = [pl.ds(pl.multiple_of(64 * r + 8 * i, 8), 8) for i in range(8)]
                tiles = [a[h, rows[i], :] for i in range(8)]
                for t in (2 * tp, 2 * tp + 1):
                    xs[r % 4, h, r // 4, 8 * t : 8 * t + 8, :] = contract(coef(h, 0, t), tiles)

    def piece(ref, tp):
        return ref.at[:, :, pl.ds(16 * tp, 16), :]

    def x_copy(d, tp):
        target = lax.rem(x + d, 4)
        return pltpu.make_async_remote_copy(
            src_ref=piece(xs.at[target], tp),
            dst_ref=piece(xr.at[d - 1], tp),
            send_sem=x_send,
            recv_sem=x_recv.at[tp],
            device_id=(z * 4 + target, ax),
            device_id_type=MESH,
        )

    for tp in range(4):
        sample(tp)
        for d in (2, 1, 3):
            x_copy(d, tp).start()

    wide = lax.broadcasted_iota(jnp.int32, (32, 256), 1)

    def collect(ref, tp, s):
        rows = pl.ds(16 * tp, 16)
        values = jnp.concatenate(
            [ref[0, :, rows, :].reshape(32, 128), ref[1, :, rows, :].reshape(32, 128)], axis=1
        )
        high = values.astype(BF16).astype(F32)
        part = 0.0
        for term in (high, values - high):
            stack = jnp.concatenate(
                [
                    jnp.where((wide >= E * c) & (wide < E * c + E), term, 0.0).astype(BF16)
                    for c in range(C)
                ],
                axis=0,
            )
            part = part + lax.dot_general(
                stack, place[s], (((1,), (1,)), ((), ())), preferred_element_type=F32
            )
        return part

    low8 = lane < 64

    def x_finish(tp):
        part = collect(xs.at[x], tp, 0)
        moved(xr.at[:, :, :, pl.ds(16 * tp, 16), :], x_send, x_recv.at[tp]).wait_recv()
        for d in (1, 3, 2):
            part = part + collect(xr.at[d - 1], tp, d)
        for c in range(C):
            for r2 in range(2):
                o = 32 * c + 16 * r2
                for v in range(2):
                    even = part[o : o + 8, 128 * v : 128 * v + 128]
                    odd = part[o + 8 : o + 16, 128 * v : 128 * v + 128]
                    zs[4 * v + r2, tp, c] = jnp.where(low8, even, pltpu.roll(odd, 64, 1))
                    zs[4 * v + 2 + r2, tp, c] = jnp.where(low8, pltpu.roll(even, 64, 1), odd)

    def z_plan(k, tp):
        long = (tp < 2) == (k == 0)
        if tp in CHAINED:
            return [(r, 1) for r in ((4, 3, 2, 1) if long else (3, 2, 1))]
        return ([(4, 2)] if long else []) + [(3, 1), (2, 2), (1, 1)]

    z_slots = {}
    z_sems = {}
    for tp in range(4):
        for k in range(2):
            for n, (reach, step) in enumerate(z_plan(k, tp)):
                z_slots[k, tp, reach] = n
                if reach > step:
                    z_sems.setdefault((k, tp, reach - step), len(z_sems))

    def z_copy(k, tp, reach):
        step = dict(z_plan(k, tp))[reach]
        way = (1, 7)[k]
        return pltpu.make_async_remote_copy(
            src_ref=zs.at[lax.rem(z + way * reach, 8), tp],
            dst_ref=zr.at[z_slots[k, tp, reach], k, tp],
            send_sem=z_send,
            recv_sem=z_recv.at[z_sems[k, tp, reach - step]] if reach > step else z_last,
            device_id=(lax.rem(z + way * step, 8) * 4 + x, ax),
            device_id_type=MESH,
        )

    def z_send_on(tp, reach):
        for k in range(2):
            plan = dict(z_plan(k, tp))
            if reach not in plan:
                continue
            coming = [z_slots[k, tp, r] for r, step in plan.items() if r - step == reach]
            if coming:
                size = len(coming)
                moved(
                    zr.at[pl.ds(coming[0], size), k, tp], z_send, z_recv.at[z_sems[k, tp, reach]]
                ).wait_recv()
                target = lax.rem(z + (1, 7)[k] * reach, 8)
                more = zr[coming[0], k, tp]
                if size > 1:
                    more = more + zr[coming[1], k, tp]
                zs[target, tp] += more
            z_copy(k, tp, reach).start()

    def z_stage(tp, n):
        if tp in CHAINED:
                rounds = [[4], [3], [2], [1]]
        else:
            rounds = [[4, 3], [2, 1], [], []]
        if 0 <= n < 4:
            for reach in rounds[n]:
                z_send_on(tp, reach)

    for n in range(4):
        for h in range(2):
            flat[128 * h : 128 * h + 128, 128 * n : 128 * n + 128] = b[
                h, 128 * n : 128 * n + 128, :
            ].T
    new_copy = pltpu.make_async_copy(flat.at[0 : C * E], new_ref, new_sem)
    new_copy.start()

    for stage in range(8):
        if stage < 4:
            x_finish(stage)
        for tp in reversed(range(4)):
            z_stage(tp, stage - tp)
    moved(zr.at[pl.ds(0, Z_ENDS // 4), 0], z_send, z_last).wait_recv()
    for tp in range(4):
        total = zs[z, tp]
        for k in range(2):
            for reach, step in z_plan(k, tp):
                if reach == step:
                    total = total + zr[z_slots[k, tp, reach], k, tp]
        sum_ref[tp] = total

    sum_copy = pltpu.make_async_copy(sum_ref, sum_hbm, state_sem.at[0])
    sum_copy.start()
    new_copy.wait()
    gather.drain()
    gather2.drain()
    moved(names_in, name_send, name_recv).wait_send()
    moved(xr, x_send, x_recv.at[0]).wait_send()
    moved(zr.at[pl.ds(0, 3), 0], z_send, z_last).wait_send()
    moved(zr.at[pl.ds(0, 4), 1], z_send, z_last).wait_send()
    sum_copy.wait()


def finish(
    rows_ref,
    sum_hbm,
    table_hbm,
    twiddle_hbm,
    new_ref,
    spec_hbm,
    rows,
    sum_ref,
    table_ref,
    twiddle_ref,
    spec_ref,
    in_sem,
    small_sem,
    out_sem,
):
    def move(k, arriving):
        part = pl.ds(48 * k, 48)
        if arriving:
            return pltpu.make_async_copy(rows_ref.at[part], rows.at[part], in_sem.at[k])
        return pltpu.make_async_copy(rows.at[part], new_ref.at[part], out_sem.at[k])

    small = [
        pltpu.make_async_copy(src, dst, small_sem.at[k])
        for k, (src, dst) in enumerate(
            ((sum_hbm, sum_ref), (table_hbm, table_ref), (twiddle_hbm, twiddle_ref))
        )
    ]
    for copy in small:
        copy.start()
    for k in range(C):
        move(k, True).start()
    for copy in small:
        copy.wait()
    for k in range(C):
        move(k, True).wait()
        move(k, False).start()
    series = sum_ref[...].reshape(4 * C * 8, 128)
    high = series.astype(BF16)
    low = (series - high.astype(F32)).astype(BF16)
    points = (
        jnp.dot(high, table_ref[0], preferred_element_type=F32)
        + jnp.dot(low, table_ref[0], preferred_element_type=F32)
        + jnp.dot(high, table_ref[1], preferred_element_type=F32)
    )
    for v in range(4):
        real, imag = 0.0, 0.0
        for t in range(8):
            span = slice(8 * C * (t // 2), 8 * C * (t // 2) + 8 * C)
            re = points[span, 256 * (t % 2) : 256 * (t % 2) + 128]
            im = points[span, 256 * (t % 2) + 128 : 256 * (t % 2) + 256]
            wr = twiddle_ref[0, t : t + 1, 128 * v : 128 * v + 128]
            wi = twiddle_ref[1, t : t + 1, 128 * v : 128 * v + 128]
            real = real + (re * wr - im * wi)
            imag = imag + (re * wi + im * wr)
        spec_ref[0, :, 128 * v : 128 * v + 128] = real
        spec_ref[1, :, 128 * v : 128 * v + 128] = imag
    spec_copy = pltpu.make_async_copy(spec_ref, spec_hbm, small_sem.at[3])
    spec_copy.start()
    spec_copy.wait()
    for k in range(C):
        move(k, False).wait()


def per_device(n_ax, state, velocity, interp_maps, neighbours, send_faces, owner_device, owner_block):
    vmem = pl.BlockSpec(memory_space=pltpu.VMEM)
    hbm = pl.BlockSpec(memory_space=pl.ANY)
    dma = pltpu.SemaphoreType.DMA
    half_nodes = pltpu.VMEM((2, 512, 128), F32)
    rows, sums = pl.pallas_call(
        functools.partial(kernel, n_ax),
        out_shape=(
            jax.ShapeDtypeStruct((C * E, 512), F32),
            jax.ShapeDtypeStruct((4, C, 8, 128), F32),
        ),
        in_specs=[hbm] * 7,
        out_specs=(hbm, hbm),
        scratch_shapes=[
            pltpu.VMEM((4, C, 8, 128), F32),
            pltpu.VMEM((256, 512), F32),
            half_nodes,
            half_nodes,
            half_nodes,
            half_nodes,
            pltpu.VMEM((3, 2, 8, 128), F32),
            pltpu.VMEM((2, 192, 128), F32),
            pltpu.VMEM((3, 256, 128), F32),
            pltpu.VMEM((3, ROWS, 128), F32),
            pltpu.VMEM((E, 128), F32),
            pltpu.VMEM((BLOCK * n_ax + 3 * ROWS, 128), F32),
            pltpu.VMEM((BLOCK * n_ax + 3 * ROWS, 128), F32),
            pltpu.VMEM((3, ROWS, 128), F32),
            pltpu.VMEM((16, 128), jnp.int32),
            pltpu.SMEM((16, 128), jnp.int32),
            pltpu.VMEM((ROWS, 128), F32),
            pltpu.VMEM((3, E), F32),
            pltpu.VMEM((192, E), F32),
            pltpu.VMEM((1, E), jnp.int32),
            pltpu.VMEM((1, E), jnp.int32),
            pltpu.VMEM((6, E), jnp.int32),
            pltpu.SMEM((1, E), jnp.int32),
            dma((6,)),
            dma,
            pltpu.VMEM((2, 384, 128), F32),
            pltpu.VMEM((2, 8, 128), F32),
            pltpu.VMEM((3, 2, 8, 128), F32),
            pltpu.VMEM((4, 256, 256), BF16),
            pltpu.VMEM((4, 2, 2, 64, 128), F32),
            pltpu.VMEM((3, 2, 2, 64, 128), F32),
            pltpu.VMEM((8, 4, C, 8, 128), F32),
            pltpu.VMEM((4, 2, 4, C, 8, 128), F32),
            dma((2,)),
            dma,
            dma((2,)),
            dma((2, 2, 4, 2)),
            dma((2,)),
            dma,
            dma,
            dma,
            dma((4,)),
            dma,
            dma((Z_STEPS,)),
            dma,
        ],
        compiler_params=pltpu.CompilerParams(
            collective_id=0, has_side_effects=True, vmem_limit_bytes=56 * 1024 * 1024
        ),
        name="advance",
    )(
        velocity.T,
        interp_maps.transpose(1, 2, 3, 0).reshape(192, E),
        owner_device.reshape(1, E),
        owner_block.reshape(1, E),
        neighbours.T,
        send_faces.reshape(1, E),
        state.transpose(1, 0, 2).reshape(C * E, 512),
    )
    new, spec = pl.pallas_call(
        finish,
        out_shape=(
            jax.ShapeDtypeStruct((C * E, 512), F32),
            jax.ShapeDtypeStruct((2, 8 * C, 512), F32),
        ),
        in_specs=[hbm] * 4,
        out_specs=(hbm, hbm),
        scratch_shapes=[
            pltpu.VMEM((C * E, 512), F32),
            pltpu.VMEM((4, C, 8, 128), F32),
            pltpu.VMEM((2, 128, 512), BF16),
            pltpu.VMEM((2, 8, 512), F32),
            pltpu.VMEM((2, 8 * C, 512), F32),
            dma((C,)),
            dma((4,)),
            dma((C,)),
        ],
        name="spectra",
    )(rows, sums, jnp.asarray(TABLES), jnp.asarray(TWIDDLE))
    return (
        new.reshape(C, E, 512).transpose(1, 0, 2),
        spec.reshape(2, C, 8, 512),
    )


def solution(mesh):
    return jax.shard_map(
        functools.partial(per_device, mesh.shape["ax"]),
        mesh=mesh,
        in_specs=(
            P(("az", "ax"), None, None),
            P(("az", "ax"), None),
            P(("az", "ax"), None, None, None),
            P(("az", "ax"), None),
            P(("az", "ax")),
            P(("az", "ax"), None),
            P(("az", "ax")),
        ),
        out_specs=(P(("az", "ax"), None, None), P(None, None, ("az", "ax"), None)),
        check_vma=False,
    )
```

```python
import functools

import jax
import jax.numpy as jnp
import ml_dtypes
import numpy as np
from jax import lax
from jax.experimental import pallas as pl
from jax.experimental.pallas import tpu as pltpu
from jax.sharding import PartitionSpec as P

MESH = pl.DeviceIdType.MESH
F32 = jnp.float32
BF16 = jnp.bfloat16
E = 48
C = 5
ROWS = 6 * E
COUNTS = (48, 48, 24)
RISING = (24, 24, 16)
FIELDS = (2, 2, 1)
STEP = 0.02
LIFT = 0.02 * 5.0


def spectral_derivative():
    points = np.cos(np.pi * np.arange(8) / 7.0)
    ends = (np.arange(8) == 0) | (np.arange(8) == 7)
    scales = np.where(ends, 2.0, 1.0)
    signs = np.where(np.arange(8) % 2 == 0, 1.0, -1.0)
    differ = points[:, None] - points[None, :]
    offdiag = (
        scales[:, None]
        / scales[None, :]
        * signs[:, None]
        * signs[None, :]
        / np.where(np.eye(8) > 0, 1.0, differ)
    )
    inner = -points / (2.0 * np.where(ends, 1.0, 1.0 - points * points))
    corner = (2.0 * 49.0 + 1.0) / 6.0
    diagonal = np.where(np.arange(8) == 0, corner, np.where(np.arange(8) == 7, -corner, inner))
    return np.where(np.eye(8) > 0, diagonal[:, None], offdiag)


DERIV = [[float(np.float32(v)) for v in row] for row in spectral_derivative()]


def dft_tables():
    j, m0 = np.meshgrid(np.arange(64), np.arange(64), indexing="ij")
    angle = (j * m0 % 64) * (2.0 * np.pi / 64)
    points = np.concatenate([np.cos(angle)] * 2 + [-np.sin(angle)] * 2, axis=1)
    table = np.zeros((2, 64, 2, 256))
    table[0, :, 0], table[1, :, 1] = points, points
    table = table.reshape(128, 512)
    high = table.astype(ml_dtypes.bfloat16)
    low = (table - high.astype(np.float64)).astype(ml_dtypes.bfloat16)
    t, m = np.meshgrid(np.arange(8), np.arange(512), indexing="ij")
    angle = (t * m % 512) * (2.0 * np.pi / 512)
    twiddle = np.stack([np.cos(angle), -np.sin(angle)]) * 512**-0.5
    return np.stack([high, low]), twiddle.astype(np.float32)


TABLES, TWIDDLE = dft_tables()


def contract(coef, tiles):
    total = coef(0) * tiles[0]
    for k in range(1, len(tiles)):
        total = total + coef(k) * tiles[k]
    return total


def kernel(
    n_ax,
    vel_hbm,
    maps_hbm,
    owner_hbm,
    block_hbm,
    nbv_hbm,
    send_hbm,
    state_ref,
    new_ref,
    sum_hbm,
    sum_ref,
    flat,
    u,
    a,
    b,
    b2,
    vel,
    mt,
    fr,
    local,
    last,
    tab_a0,
    tab_b0,
    tab_c0,
    tab_a1,
    tab_b1,
    tab_c1,
    gat,
    where_v,
    where,
    upper,
    vel_ref,
    maps_ref,
    owner_ref,
    block_ref,
    nbv_ref,
    send_ref,
    wt,
    names,
    names_in,
    place,
    place_c,
    xs,
    xc,
    xr,
    xrc,
    zs,
    zr,
    in_sem,
    where_sem,
    state_sem,
    new_sem,
    ag_send,
    y_recv,
    sib_recv,
    name_send,
    name_recv,
    x_send,
    x_recv,
    z_send,
    z_recv,
    z_last,
):
    az, ax = lax.axis_index("az"), lax.axis_index("ax")
    z, x = az // 4, az % 4
    up, dn = lax.rem(ax + 2, n_ax), lax.rem(ax + n_ax - 2, n_ax)
    up2, dn2 = lax.rem(ax + 4, n_ax), lax.rem(ax + n_ax - 4, n_ax)
    sib = ax + 1 - 2 * lax.rem(ax, 2)
    tabs = ((tab_a0, tab_b0, tab_c0), (tab_a1, tab_b1, tab_c1))

    state_copies = [
        pltpu.make_async_copy(
            state_ref.at[pl.ds(96 * G, E * FIELDS[G])],
            flat.at[G, pl.ds(0, E * FIELDS[G])],
            state_sem.at[G],
        )
        for G in range(3)
    ]
    operand_copies = [
        pltpu.make_async_copy(src, dst, in_sem.at[n])
        for n, (src, dst) in enumerate(
            (
                (send_hbm, send_ref),
                (vel_hbm, vel_ref),
                (owner_hbm, owner_ref),
                (block_hbm, block_ref),
                (nbv_hbm, nbv_ref),
                (maps_hbm, maps_ref),
            )
        )
    ]
    for copy in state_copies + operand_copies:
        copy.start()
    barrier = pltpu.get_barrier_semaphore()
    for peer in (up, dn, up2, dn2, sib):
        pl.semaphore_signal(barrier, inc=1, device_id=(az, peer), device_id_type=MESH)
    for d in range(1, 4):
        pl.semaphore_signal(
            barrier, inc=1, device_id=(z * 4 + lax.rem(x + d, 4), ax), device_id_type=MESH
        )
    for d in (1, 2, 6, 7):
        pl.semaphore_signal(
            barrier, inc=1, device_id=(lax.rem(z + d, 8) * 4 + x, ax), device_id_type=MESH
        )

    def low_half(rows):
        return lax.broadcasted_iota(jnp.int32, (rows, 128), 1) < 64

    def moved(ref, send, recv):
        return pltpu.make_async_remote_copy(
            src_ref=ref,
            dst_ref=ref,
            send_sem=send,
            recv_sem=recv,
            device_id=(az, sib),
            device_id_type=MESH,
        )

    def load(G):
        width = E * FIELDS[G]
        flat[G, width:128] = jnp.zeros((128 - width, 512), F32)
        state_copies[G].wait()
        for n in range(4):
            u[G, 128 * n : 128 * n + 128, :] = flat[G, :, 128 * n : 128 * n + 128].T

    def face_pair(ref, G, pair):
        if pair == 0:
            return jnp.concatenate([ref[G, 0:64, :], ref[G, 448:512, :]], axis=0)
        if pair == 1:
            return jnp.concatenate(
                [ref[G, 64 * i + o : 64 * i + o + 8, :] for o in (0, 56) for i in range(8)], axis=0
            )
        return jnp.concatenate(
            [ref[G, pl.ds(0, 64, stride=8), :], ref[G, pl.ds(7, 64, stride=8), :]], axis=0
        )

    def publish(ref, g, G):
        table = tabs[g][G]
        low = low_half(48)
        for pair in range(3):
            turned = face_pair(ref, G, pair).T
            first = turned[0:48]
            second = turned[48:96]
            even = jnp.where(low, first, pltpu.roll(second, 64, 1))
            odd = jnp.where(low, pltpu.roll(first, 64, 1), second)
            for o, rows in ((0, even), (1, odd)):
                f = 2 * pair + o
                local[G, pl.ds(f, 48, stride=6), :] = rows
                table[pl.ds(f, 48, stride=6), :] = rows
        own = pl.multiple_of(ROWS + COUNTS[G] * ax, 8)

        @pl.loop(0, 6)
        def _(i):
            for k in range(8):
                s = 8 * i + k
                row = local[G, pl.ds(send_ref[0, s], 1), :]
                if G < 2:
                    table[pl.ds(own + s, 1), :] = row
                else:
                    last[pl.ds(s, 1), :] = row

        if G == 2:
            table[pl.ds(own, 24), :] = jnp.where(
                low_half(24), last[0:24, :], pltpu.roll(last[24:48, :], 64, 1)
            )

    def ag_copy(g, source, G, part, target, recv):
        start, count = 0, COUNTS[G]
        if part == 0:
            count = RISING[G]
        if part == 1:
            start, count = RISING[G], COUNTS[G] - RISING[G]
        rows = pl.ds(pl.multiple_of(ROWS + COUNTS[G] * source + start, 8), count)
        return pltpu.make_async_remote_copy(
            src_ref=tabs[g][G].at[rows, :],
            dst_ref=tabs[g][G].at[rows, :],
            send_sem=ag_send.at[g, G],
            recv_sem=recv,
            device_id=(az, target),
            device_id_type=MESH,
        )

    def behind(way, h):
        return lax.rem(ax + (n_ax - 2 * h if way == 0 else 2 * h), n_ax)

    WHOLE = 2
    ways = ((0, up, up2), (1, dn, dn2))

    def share(g, source, G, part):
        ag_copy(g, source, G, part, sib, sib_recv.at[g, G]).start()

    def ag_start(g, G):
        for way, _, two in ways:
            ag_copy(g, ax, G, WHOLE, two, y_recv.at[g, G, way, 1]).start()
        for way, one, _ in ways:
            ag_copy(g, ax, G, WHOLE, one, y_recv.at[g, G, way, 0]).start()
        share(g, ax, G, WHOLE)

    def ag_take(g, G, h):
        for way, one, two in ways:
            source = behind(way, h)
            part = WHOLE if h < 4 else way
            ag_copy(g, source, G, part, one, y_recv.at[g, G, way, h - 1]).wait_recv()
            if h == 2:
                ag_copy(g, source, G, way, two, y_recv.at[g, G, way, 3]).start()
                ag_copy(g, source, G, WHOLE, one, y_recv.at[g, G, way, 2]).start()
            share(g, source, G, part)

    def ag_rest(g, G):
        for h in (1, 3, 4):
            ag_take(g, G, h)
        moved(
            tabs[g][G].at[pl.ds(0, 8 * COUNTS[G]), :], ag_send.at[g, G], sib_recv.at[g, G]
        ).wait_recv()

    def along_x(src, dst, G):
        @pl.loop(0, 8)
        def _(y):
            rows = [pl.ds(pl.multiple_of(64 * i + 8 * y, 8), 8) for i in range(8)]
            tiles = [src[G, rows[i], :] for i in range(8)]
            v = vel[0]
            for i in range(8):
                dst[G, rows[i], :] = tiles[i] + v * contract(lambda k: DERIV[i][k], tiles)

    def along_yz(src, dst, G):
        @pl.loop(0, 8)
        def _(i):
            rows = [pl.ds(pl.multiple_of(64 * i + 8 * y, 8), 8) for y in range(8)]
            tiles = [src[G, rows[y], :] for y in range(8)]
            v = vel[1]
            for y in range(8):
                dst[G, rows[y], :] += v * contract(lambda k: DERIV[y][k], tiles)
            cols = [pl.ds(64 * i + q, 8, stride=8) for q in range(8)]
            tiles = [src[G, cols[q], :] for q in range(8)]
            v = vel[2]
            for q in range(8):
                dst[G, cols[q], :] += v * contract(lambda k: DERIV[q][k], tiles)

    def lift(dst, G, value, scale):
        dst[G, 0:64, :] += scale * value(0)
        dst[G, 448:512, :] += scale * value(1)
        for f, o in ((2, 0), (3, 56)):
            rows = scale * value(f)
            for i in range(8):
                dst[G, 64 * i + o : 64 * i + o + 8, :] += rows[8 * i : 8 * i + 8]
        dst[G, pl.ds(0, 64, stride=8), :] += scale * value(4)
        dst[G, pl.ds(7, 64, stride=8), :] += scale * value(5)

    def advance(src, dst, G):
        along_x(src, dst, G)
        along_yz(src, dst, G)

        def own_face(f):
            return face_pair(src, G, f // 2)[64 * (f % 2) : 64 * (f % 2) + 64]

        lift(dst, G, own_face, -LIFT)

    def facing(g, G, dst, scale):
        table = tabs[g][G]

        @pl.loop(0, E // 2)
        def _(i):
            for k in range(2):
                e = 2 * i + k
                for f in range(6):
                    row = where[8 * (G // 2) + f, e]
                    gat[pl.ds(f * E + e, 1), :] = table[pl.ds(row, 1), :]

        def got(f):
            rows = gat[f * E : f * E + E, :]
            if G < 2:
                return rows
            return jnp.where(upper[f * E : f * E + E, :] > 0.5, pltpu.roll(rows, 64, 1), rows)

        low = low_half(48)
        for pair in range(3):
            first, second = got(2 * pair), got(2 * pair + 1)
            fr[pair, 0:48, :] = jnp.where(low, first, pltpu.roll(second, 64, 1))
            fr[pair, 48:96, :] = (
                jnp.where(low, pltpu.roll(first, 64, 1), second)
                if G < 2
                else jnp.zeros((48, 128), F32)
            )
            wt[128 * pair : 128 * pair + 128, :] = fr[pair].T
        lift(dst, G, lambda f: wt[64 * f : 64 * f + 64, :], scale)

    fr[:, 96:128, :] = jnp.zeros((3, 32, 128), F32)
    for G in range(3):
        load(G)
        if G == 0:
            operand_copies[0].wait()
        publish(u, 0, G)
        if G == 0:
            pl.semaphore_wait(barrier, 12)
        ag_start(0, G)
    for copy in operand_copies[1:]:
        copy.wait()

    lane = lax.broadcasted_iota(jnp.int32, (E, 128), 1)
    element = lax.broadcasted_iota(jnp.int32, (E, 128), 0)
    spread = ((lane == element) | (lane == element + E)).astype(F32)

    def over_lanes(rows):
        return jnp.dot(rows, spread, precision=lax.Precision.HIGHEST, preferred_element_type=F32)

    speeds = over_lanes(-STEP * vel_ref[...])
    block = block_ref[...]
    label = lax.rem(block, 4) * 64 + owner_ref[...] * 2 + block // 4
    names[...] = jnp.broadcast_to(over_lanes(label.astype(F32)), (8, 128))
    for d in range(3):
        vel[d] = jnp.broadcast_to(speeds[d : d + 1], (8, 128))
    for d in range(1, 4):
        pltpu.make_async_remote_copy(
            src_ref=names,
            dst_ref=names_in.at[d - 1],
            send_sem=name_send,
            recv_sem=name_recv,
            device_id=(z * 4 + lax.rem(x + d, 4), ax),
            device_id_type=MESH,
        ).start()

    row = nbv_ref[...]
    slot = row - ROWS
    device = slot // E
    slot = slot - E * device
    upper_row = (row >= ROWS) & (slot >= 24)
    where_v[0:6, 0:E] = row
    where_v[8:14, 0:E] = jnp.where(
        row < ROWS, row, ROWS + 24 * device + slot - jnp.where(upper_row, 24, 0)
    )
    where_copy = pltpu.make_async_copy(where_v, where, where_sem)
    where_copy.start()
    folds = upper_row.astype(F32)
    diagonal = lax.broadcasted_iota(jnp.int32, (E, E), 0) == lax.broadcasted_iota(
        jnp.int32, (E, E), 1
    )
    for f in range(6):
        upper[f * E : f * E + E, :] = jnp.dot(
            jnp.where(diagonal, folds[f : f + 1, :], 0.0),
            jnp.ones((E, 128), F32),
            preferred_element_type=F32,
        )

    def coef(which, out):
        return lambda k: mt[pl.ds(64 * which + 8 * out + k, 1), :]

    def sample(G):
        @pl.loop(0, 8)
        def _(y):
            rows = [pl.ds(pl.multiple_of(64 * i + 8 * y, 8), 8) for i in range(8)]
            tiles = [b[G, rows[i], :] for i in range(8)]
            for r in range(8):
                b2[rows[r], :] = contract(coef(1, r), tiles)

        @pl.loop(0, 8)
        def _(r):
            cols = [pl.ds(64 * r + q, 8, stride=8) for q in range(8)]
            tiles = [b2[cols[q], :] for q in range(8)]
            for q in range(8):
                a[G, cols[q], :] = contract(coef(2, q), tiles)

        @pl.loop(0, 4)
        def _(r):
            low = low_half(8)
            for t in range(8):
                both = []
                for r2 in range(2):
                    tiles = [
                        a[G, pl.ds(pl.multiple_of(64 * (r + 4 * r2) + 8 * i, 8), 8), :]
                        for i in range(8)
                    ]
                    both.append(contract(coef(0, t), tiles))
                if G < 2:
                    for r2 in range(2):
                        xs[r, G, r2, 8 * t : 8 * t + 8, :] = both[r2]
                else:
                    xc[r, 8 * t : 8 * t + 8, :] = jnp.where(
                        low, both[0], pltpu.roll(both[1], 64, 1)
                    )

    def x_send_all(G):
        for d in (2, 1, 3):
            target = lax.rem(x + d, 4)
            pltpu.make_async_remote_copy(
                src_ref=xs.at[target, G] if G < 2 else xc.at[target],
                dst_ref=xr.at[G, d - 1] if G < 2 else xrc.at[d - 1],
                send_sem=x_send,
                recv_sem=x_recv.at[G],
                device_id=(z * 4 + target, ax),
                device_id_type=MESH,
            ).start()

    def set_places():
        moved(names_in, name_send, name_recv).wait_recv()
        rows = lax.broadcasted_iota(jnp.int32, (256, 128), 0)
        lanes = lax.broadcasted_iota(jnp.int32, (1, 128), 1)
        for s in range(4):
            name = (names[0:1, :] if s == 0 else names_in[s - 1, 0:1, :]).astype(jnp.int32)
            place[:, 128 * s : 128 * s + 128] = (rows == name).astype(F32).astype(BF16)
            name = jnp.where(
                lanes < 64, name, pltpu.roll(names[0:1, :] if s == 0 else names_in[s - 1, 0:1, :], 64, 1).astype(jnp.int32)
            )
            place_c[:, 128 * s : 128 * s + 128] = (rows == name).astype(F32).astype(BF16)

    low8 = low_half(8)

    def x_finish(G):
        if G < 2:
            moved(xr.at[G], x_send, x_recv.at[G]).wait_recv()
            sources = [xs[x, G]] + [xr[G, d] for d in range(3)]
            values = jnp.concatenate([v.reshape(128, 128) for v in sources], axis=1)
            width = E
        else:
            moved(xrc, x_send, x_recv.at[G]).wait_recv()
            values = jnp.concatenate([xc[x]] + [xrc[d] for d in range(3)], axis=1)
            width = 64
        names_of = place if G < 2 else place_c
        wide = lax.rem(lax.broadcasted_iota(jnp.int32, values.shape, 1), 128)
        high = values.astype(BF16).astype(F32)
        part = 0.0
        for term in (high, values - high):
            stack = jnp.concatenate(
                [
                    jnp.where((wide >= width * k) & (wide < width * k + E), term, 0.0).astype(BF16)
                    for k in range(2)
                ],
                axis=0,
            )
            part = part + lax.dot_general(
                stack, names_of[...], (((1,), (1,)), ((), ())), preferred_element_type=F32
            )
        for c in range(FIELDS[G]):
            for r2 in range(2):
                for tp in range(4):
                    o = 128 * c + 64 * r2 + 16 * tp
                    for v in range(2):
                        even = part[o : o + 8, 128 * v : 128 * v + 128]
                        odd = part[o + 8 : o + 16, 128 * v : 128 * v + 128]
                        zs[4 * v + r2, G, tp // 2, c, tp % 2] = jnp.where(
                            low8, even, pltpu.roll(odd, 64, 1)
                        )
                        zs[4 * v + 2 + r2, G, tp // 2, c, tp % 2] = jnp.where(
                            low8, pltpu.roll(even, 64, 1), odd
                        )

    def z_copy(kind, k, G, half):
        reach, step = ((4, 2), (3, 1), (2, 2), (1, 1))[kind]
        way = (1, 7)[k]
        fields = pl.ds(0, FIELDS[G])
        return pltpu.make_async_remote_copy(
            src_ref=zs.at[lax.rem(z + way * reach, 8), G, half, fields],
            dst_ref=zr.at[G, half, k, kind, fields],
            send_sem=z_send,
            recv_sem=z_recv.at[G, half, k] if kind < 2 else z_last.at[G, half],
            device_id=(lax.rem(z + way * step, 8) * 4 + x, ax),
            device_id_type=MESH,
        )

    def z_first(G):
        for half in range(2):
            z_copy(0, half, G, half).start()
            for k in range(2):
                z_copy(1, k, G, half).start()

    def z_second(G):
        fields = pl.ds(0, FIELDS[G])
        for half in range(2):
            for k in (1 - half, half):
                target = lax.rem(z + (2, 6)[k], 8)
                least = 0 if k == half else 1
                moved(
                    zr.at[G, half, k, pl.ds(least, 2 - least), fields],
                    z_send,
                    z_recv.at[G, half, k],
                ).wait_recv()
                more = zr[G, half, k, 1, fields]
                if k == half:
                    more = more + zr[G, half, k, 0, fields]
                zs[target, G, half, fields] += more
                z_copy(2, k, G, half).start()
        for half in range(2):
            for k in range(2):
                z_copy(3, k, G, half).start()

    def new_rows(G):
        for n in range(4):
            flat[G, :, 128 * n : 128 * n + 128] = b[G, 128 * n : 128 * n + 128, :].T
        copy = pltpu.make_async_copy(
            flat.at[G, pl.ds(0, E * FIELDS[G])],
            new_ref.at[pl.ds(96 * G, E * FIELDS[G])],
            new_sem.at[G],
        )
        copy.start()
        return copy

    def first_section(G):
        facing(0, G, a, LIFT)
        publish(a, 1, G)
        ag_start(1, G)

    def second_base(G):
        advance(a, b, G)
        b[G] = 0.5 * (u[G] + b[G])

    def second_section(G):
        facing(1, G, b, 0.5 * LIFT)

    for G in range(3):
        advance(u, a, G)
    where_copy.wait()
    for G in range(3):
        ag_take(0, G, 2)
    ag_rest(0, 0)
    first_section(0)
    ag_rest(0, 1)
    first_section(1)
    ag_rest(0, 2)
    first_section(2)
    ag_take(1, 0, 2)
    second_base(0)
    mt[...] = over_lanes(maps_ref[...])
    ag_take(1, 1, 2)
    second_base(1)
    ag_take(1, 2, 2)
    second_base(2)
    set_places()
    for G in range(3):
        ag_rest(1, G)
        second_section(G)
        sample(G)
        x_send_all(G)
        if G == 2:
            x_finish(0)
            z_first(0)
    x_finish(1)
    z_first(1)
    new_copies = [new_rows(G) for G in range(3)]
    z_second(0)
    x_finish(2)
    z_first(2)
    z_second(1)
    z_second(2)
    for G in range(3):
        for half in range(2):
            moved(
                zr.at[G, half, :, pl.ds(2, 2), pl.ds(0, FIELDS[G])], z_send, z_last.at[G, half]
            ).wait_recv()
    for G in range(3):
        for half in range(2):
            for c in range(FIELDS[G]):
                total = zs[z, G, half, c]
                for kind in (3, 2):
                    for k in range(2):
                        total = total + zr[G, half, k, kind, c]
                for tp in range(2):
                    sum_ref[2 * half + tp, 2 * G + c] = total[tp]

    sum_copy = pltpu.make_async_copy(sum_ref, sum_hbm, in_sem.at[0])
    sum_copy.start()
    for copy in new_copies:
        copy.wait()
    for g in range(2):
        for G in range(3):
            moved(
                tabs[g][G].at[pl.ds(0, 15 * COUNTS[G]), :], ag_send.at[g, G], sib_recv.at[g, G]
            ).wait_send()
    moved(names_in, name_send, name_recv).wait_send()
    for G in range(2):
        moved(xr.at[G], x_send, x_recv.at[0]).wait_send()
    moved(xrc, x_send, x_recv.at[0]).wait_send()
    for G in range(3):
        for half in range(2):
            fields = pl.ds(0, FIELDS[G])
            moved(
                zr.at[G, half, :, pl.ds(1, 3), fields], z_send, z_last.at[0, 0]
            ).wait_send()
            moved(zr.at[G, half, 0, 0, fields], z_send, z_last.at[0, 0]).wait_send()
    sum_copy.wait()


def finish(
    rows_ref,
    sum_hbm,
    table_hbm,
    twiddle_hbm,
    new_ref,
    spec_hbm,
    rows,
    sum_ref,
    table_ref,
    twiddle_ref,
    spec_ref,
    in_sem,
    small_sem,
    out_sem,
):
    def move(k, arriving):
        part = pl.ds(48 * k, 48)
        if arriving:
            return pltpu.make_async_copy(rows_ref.at[part], rows.at[part], in_sem.at[k])
        return pltpu.make_async_copy(rows.at[part], new_ref.at[part], out_sem.at[k])

    small = [
        pltpu.make_async_copy(src, dst, small_sem.at[k])
        for k, (src, dst) in enumerate(
            ((sum_hbm, sum_ref), (table_hbm, table_ref), (twiddle_hbm, twiddle_ref))
        )
    ]
    for copy in small:
        copy.start()
    for k in range(C):
        move(k, True).start()
    for copy in small:
        copy.wait()
    for k in range(C):
        move(k, True).wait()
        move(k, False).start()
    series = sum_ref[...].reshape(4 * C * 8, 128)
    high = series.astype(BF16)
    low = (series - high.astype(F32)).astype(BF16)
    points = (
        jnp.dot(high, table_ref[0], preferred_element_type=F32)
        + jnp.dot(low, table_ref[0], preferred_element_type=F32)
        + jnp.dot(high, table_ref[1], preferred_element_type=F32)
    )
    for v in range(4):
        real, imag = 0.0, 0.0
        for t in range(8):
            span = slice(8 * C * (t // 2), 8 * C * (t // 2) + 8 * C)
            re = points[span, 256 * (t % 2) : 256 * (t % 2) + 128]
            im = points[span, 256 * (t % 2) + 128 : 256 * (t % 2) + 256]
            wr = twiddle_ref[0, t : t + 1, 128 * v : 128 * v + 128]
            wi = twiddle_ref[1, t : t + 1, 128 * v : 128 * v + 128]
            real = real + (re * wr - im * wi)
            imag = imag + (re * wi + im * wr)
        spec_ref[0, :, 128 * v : 128 * v + 128] = real
        spec_ref[1, :, 128 * v : 128 * v + 128] = imag
    spec_copy = pltpu.make_async_copy(spec_ref, spec_hbm, small_sem.at[3])
    spec_copy.start()
    spec_copy.wait()
    for k in range(C):
        move(k, False).wait()


def per_device(n_ax, state, velocity, interp_maps, neighbours, send_faces, owner_device, owner_block):
    vmem = pl.BlockSpec(memory_space=pltpu.VMEM)
    hbm = pl.BlockSpec(memory_space=pl.ANY)
    dma = pltpu.SemaphoreType.DMA
    nodes = pltpu.VMEM((3, 512, 128), F32)
    rows, sums = pl.pallas_call(
        functools.partial(kernel, n_ax),
        out_shape=(
            jax.ShapeDtypeStruct((C * E, 512), F32),
            jax.ShapeDtypeStruct((4, C, 8, 128), F32),
        ),
        in_specs=[hbm] * 7,
        out_specs=(hbm, hbm),
        scratch_shapes=[
            pltpu.VMEM((4, C, 8, 128), F32),
            pltpu.VMEM((3, 128, 512), F32),
            nodes,
            nodes,
            nodes,
            pltpu.VMEM((512, 128), F32),
            pltpu.VMEM((3, 8, 128), F32),
            pltpu.VMEM((192, 128), F32),
            pltpu.VMEM((3, 128, 128), F32),
            pltpu.VMEM((3, ROWS, 128), F32),
            pltpu.VMEM((E, 128), F32),
            *[pltpu.VMEM((ROWS + n * n_ax, 128), F32) for n in COUNTS * 2],
            pltpu.VMEM((ROWS, 128), F32),
            pltpu.VMEM((16, 128), jnp.int32),
            pltpu.SMEM((16, 128), jnp.int32),
            pltpu.VMEM((ROWS, 128), F32),
            pltpu.VMEM((3, E), F32),
            pltpu.VMEM((192, E), F32),
            pltpu.VMEM((1, E), jnp.int32),
            pltpu.VMEM((1, E), jnp.int32),
            pltpu.VMEM((6, E), jnp.int32),
            pltpu.SMEM((1, E), jnp.int32),
            pltpu.VMEM((384, 128), F32),
            pltpu.VMEM((8, 128), F32),
            pltpu.VMEM((3, 8, 128), F32),
            pltpu.VMEM((256, 512), BF16),
            pltpu.VMEM((256, 512), BF16),
            pltpu.VMEM((4, 2, 2, 64, 128), F32),
            pltpu.VMEM((4, 64, 128), F32),
            pltpu.VMEM((2, 3, 2, 64, 128), F32),
            pltpu.VMEM((3, 64, 128), F32),
            pltpu.VMEM((8, 3, 2, 2, 2, 8, 128), F32),
            pltpu.VMEM((3, 2, 2, 4, 2, 2, 8, 128), F32),
            dma((6,)),
            dma,
            dma((3,)),
            dma((3,)),
            dma((2, 3)),
            dma((2, 3, 2, 4)),
            dma((2, 3)),
            dma,
            dma,
            dma,
            dma((3,)),
            dma,
            dma((3, 2, 2)),
            dma((3, 2)),
        ],
        compiler_params=pltpu.CompilerParams(
            collective_id=0, has_side_effects=True, vmem_limit_bytes=56 * 1024 * 1024
        ),
        name="advance",
    )(
        velocity.T,
        interp_maps.transpose(1, 2, 3, 0).reshape(192, E),
        owner_device.reshape(1, E),
        owner_block.reshape(1, E),
        neighbours.T,
        send_faces.reshape(1, E),
        state.transpose(1, 0, 2).reshape(C * E, 512),
    )
    new, spec = pl.pallas_call(
        finish,
        out_shape=(
            jax.ShapeDtypeStruct((C * E, 512), F32),
            jax.ShapeDtypeStruct((2, 8 * C, 512), F32),
        ),
        in_specs=[hbm] * 4,
        out_specs=(hbm, hbm),
        scratch_shapes=[
            pltpu.VMEM((C * E, 512), F32),
            pltpu.VMEM((4, C, 8, 128), F32),
            pltpu.VMEM((2, 128, 512), BF16),
            pltpu.VMEM((2, 8, 512), F32),
            pltpu.VMEM((2, 8 * C, 512), F32),
            dma((C,)),
            dma((4,)),
            dma((C,)),
        ],
        name="spectra",
    )(rows, sums, jnp.asarray(TABLES), jnp.asarray(TWIDDLE))
    return (
        new.reshape(C, E, 512).transpose(1, 0, 2),
        spec.reshape(2, C, 8, 512),
    )


def solution(mesh):
    return jax.shard_map(
        functools.partial(per_device, mesh.shape["ax"]),
        mesh=mesh,
        in_specs=(
            P(("az", "ax"), None, None),
            P(("az", "ax"), None),
            P(("az", "ax"), None, None, None),
            P(("az", "ax"), None),
            P(("az", "ax")),
            P(("az", "ax"), None),
            P(("az", "ax")),
        ),
        out_specs=(P(("az", "ax"), None, None), P(None, None, ("az", "ax"), None)),
        check_vma=False,
    )
```

```python
import functools

import jax
import jax.numpy as jnp
import ml_dtypes
import numpy as np
from jax import lax
from jax.experimental import pallas as pl
from jax.experimental.pallas import tpu as pltpu
from jax.sharding import PartitionSpec as P

MESH = pl.DeviceIdType.MESH
F32 = jnp.float32
BF16 = jnp.bfloat16
E = 48
C = 5
ROWS = 6 * E
COUNTS = (48, 48, 24)
RISING = (24, 24, 16)
FIELDS = (2, 2, 1)
ORDER = (2, 0, 1)
STEP = 0.02
LIFT = 0.02 * 5.0


def spectral_derivative():
    points = np.cos(np.pi * np.arange(8) / 7.0)
    ends = (np.arange(8) == 0) | (np.arange(8) == 7)
    scales = np.where(ends, 2.0, 1.0)
    signs = np.where(np.arange(8) % 2 == 0, 1.0, -1.0)
    differ = points[:, None] - points[None, :]
    offdiag = (
        scales[:, None]
        / scales[None, :]
        * signs[:, None]
        * signs[None, :]
        / np.where(np.eye(8) > 0, 1.0, differ)
    )
    inner = -points / (2.0 * np.where(ends, 1.0, 1.0 - points * points))
    corner = (2.0 * 49.0 + 1.0) / 6.0
    diagonal = np.where(np.arange(8) == 0, corner, np.where(np.arange(8) == 7, -corner, inner))
    return np.where(np.eye(8) > 0, diagonal[:, None], offdiag)


DERIV = [[float(np.float32(v)) for v in row] for row in spectral_derivative()]


def dft_tables():
    j, m0 = np.meshgrid(np.arange(64), np.arange(64), indexing="ij")
    angle = (j * m0 % 64) * (2.0 * np.pi / 64)
    points = np.concatenate([np.cos(angle)] * 2 + [-np.sin(angle)] * 2, axis=1)
    table = np.zeros((2, 64, 2, 256))
    table[0, :, 0], table[1, :, 1] = points, points
    table = table.reshape(128, 512)
    high = table.astype(ml_dtypes.bfloat16)
    low = (table - high.astype(np.float64)).astype(ml_dtypes.bfloat16)
    t, m = np.meshgrid(np.arange(8), np.arange(512), indexing="ij")
    angle = (t * m % 512) * (2.0 * np.pi / 512)
    twiddle = np.stack([np.cos(angle), -np.sin(angle)]) * 512**-0.5
    return np.stack([high, low]), twiddle.astype(np.float32)


TABLES, TWIDDLE = dft_tables()


def contract(coef, tiles):
    total = coef(0) * tiles[0]
    for k in range(1, len(tiles)):
        total = total + coef(k) * tiles[k]
    return total


def kernel(
    n_ax,
    vel_hbm,
    maps_hbm,
    owner_hbm,
    block_hbm,
    nbv_hbm,
    send_hbm,
    state_ref,
    table_hbm,
    twiddle_hbm,
    new_ref,
    sum_ref,
    table_ref,
    twiddle_ref,
    flat,
    u,
    a,
    b,
    b2,
    vel,
    mt,
    fr,
    local,
    last,
    tab_a0,
    tab_b0,
    tab_c0,
    tab_a1,
    tab_b1,
    tab_c1,
    gat,
    where_v,
    where,
    upper,
    vel_ref,
    maps_ref,
    owner_ref,
    block_ref,
    nbv_ref,
    send_ref,
    wt,
    names,
    names_in,
    place,
    place_c,
    xs,
    xc,
    xr,
    xrc,
    zs,
    zr,
    in_sem,
    where_sem,
    state_sem,
    ag_send,
    y_recv,
    sib_recv,
    name_send,
    name_recv,
    x_send,
    x_recv,
    z_send,
    z_recv,
    z_last,
):
    az, ax = lax.axis_index("az"), lax.axis_index("ax")
    z, x = az // 4, az % 4
    up, dn = lax.rem(ax + 2, n_ax), lax.rem(ax + n_ax - 2, n_ax)
    up2, dn2 = lax.rem(ax + 4, n_ax), lax.rem(ax + n_ax - 4, n_ax)
    sib = ax + 1 - 2 * lax.rem(ax, 2)
    tabs = ((tab_a0, tab_b0, tab_c0), (tab_a1, tab_b1, tab_c1))

    state_copies = [
        pltpu.make_async_copy(
            state_ref.at[pl.ds(96 * G, E * FIELDS[G])],
            flat.at[G, pl.ds(0, E * FIELDS[G])],
            state_sem.at[G],
        )
        for G in range(3)
    ]
    operand_copies = [
        pltpu.make_async_copy(src, dst, in_sem.at[n])
        for n, (src, dst) in enumerate(
            (
                (send_hbm, send_ref),
                (vel_hbm, vel_ref),
                (owner_hbm, owner_ref),
                (block_hbm, block_ref),
                (nbv_hbm, nbv_ref),
                (maps_hbm, maps_ref),
                (table_hbm, table_ref),
                (twiddle_hbm, twiddle_ref),
            )
        )
    ]
    for copy in state_copies + operand_copies:
        copy.start()
    barrier = pltpu.get_barrier_semaphore()
    for peer in (up, dn, up2, dn2, sib):
        pl.semaphore_signal(barrier, inc=1, device_id=(az, peer), device_id_type=MESH)
    for d in range(1, 4):
        pl.semaphore_signal(
            barrier, inc=1, device_id=(z * 4 + lax.rem(x + d, 4), ax), device_id_type=MESH
        )
    for d in (1, 2, 6, 7):
        pl.semaphore_signal(
            barrier, inc=1, device_id=(lax.rem(z + d, 8) * 4 + x, ax), device_id_type=MESH
        )

    def low_half(rows):
        return lax.broadcasted_iota(jnp.int32, (rows, 128), 1) < 64

    def moved(ref, send, recv):
        return pltpu.make_async_remote_copy(
            src_ref=ref,
            dst_ref=ref,
            send_sem=send,
            recv_sem=recv,
            device_id=(az, sib),
            device_id_type=MESH,
        )

    def load(G):
        width = E * FIELDS[G]
        flat[G, width:128] = jnp.zeros((128 - width, 512), F32)
        state_copies[G].wait()
        for n in range(4):
            u[G, 128 * n : 128 * n + 128, :] = flat[G, :, 128 * n : 128 * n + 128].T

    def face_pair(ref, G, pair):
        if pair == 0:
            return jnp.concatenate([ref[G, 0:64, :], ref[G, 448:512, :]], axis=0)
        if pair == 1:
            return jnp.concatenate(
                [ref[G, 64 * i + o : 64 * i + o + 8, :] for o in (0, 56) for i in range(8)], axis=0
            )
        return jnp.concatenate(
            [ref[G, pl.ds(0, 64, stride=8), :], ref[G, pl.ds(7, 64, stride=8), :]], axis=0
        )

    def publish(ref, g, G):
        table = tabs[g][G]
        low = low_half(48)
        for pair in range(3):
            turned = face_pair(ref, G, pair).T
            first = turned[0:48]
            second = turned[48:96]
            even = jnp.where(low, first, pltpu.roll(second, 64, 1))
            odd = jnp.where(low, pltpu.roll(first, 64, 1), second)
            for o, rows in ((0, even), (1, odd)):
                f = 2 * pair + o
                local[G, pl.ds(f, 48, stride=6), :] = rows
                table[pl.ds(f, 48, stride=6), :] = rows
        own = pl.multiple_of(ROWS + COUNTS[G] * ax, 8)

        @pl.loop(0, 6)
        def _(i):
            for k in range(8):
                s = 8 * i + k
                row = local[G, pl.ds(send_ref[0, s], 1), :]
                if G < 2:
                    table[pl.ds(own + s, 1), :] = row
                else:
                    last[pl.ds(s, 1), :] = row

        if G == 2:
            table[pl.ds(own, 24), :] = jnp.where(
                low_half(24), last[0:24, :], pltpu.roll(last[24:48, :], 64, 1)
            )

    def ag_copy(g, source, G, part, target, recv):
        start, count = 0, COUNTS[G]
        if part == 0:
            count = RISING[G]
        if part == 1:
            start, count = RISING[G], COUNTS[G] - RISING[G]
        rows = pl.ds(pl.multiple_of(ROWS + COUNTS[G] * source + start, 8), count)
        return pltpu.make_async_remote_copy(
            src_ref=tabs[g][G].at[rows, :],
            dst_ref=tabs[g][G].at[rows, :],
            send_sem=ag_send.at[g, G],
            recv_sem=recv,
            device_id=(az, target),
            device_id_type=MESH,
        )

    def behind(way, h):
        return lax.rem(ax + (n_ax - 2 * h if way == 0 else 2 * h), n_ax)

    WHOLE = 2
    ways = ((0, up, up2), (1, dn, dn2))

    def share(g, source, G, part):
        ag_copy(g, source, G, part, sib, sib_recv.at[g, G]).start()

    def ag_start(g, G):
        for way, _, two in ways:
            ag_copy(g, ax, G, WHOLE, two, y_recv.at[g, G, way, 1]).start()
        for way, one, _ in ways:
            ag_copy(g, ax, G, WHOLE, one, y_recv.at[g, G, way, 0]).start()
        share(g, ax, G, WHOLE)

    def ag_take(g, G, h):
        for way, one, two in ways:
            source = behind(way, h)
            part = WHOLE if h < 4 else way
            ag_copy(g, source, G, part, one, y_recv.at[g, G, way, h - 1]).wait_recv()
            if h == 2:
                ag_copy(g, source, G, way, two, y_recv.at[g, G, way, 3]).start()
                ag_copy(g, source, G, WHOLE, one, y_recv.at[g, G, way, 2]).start()
            share(g, source, G, part)

    def ag_rest(g, G):
        for h in (1, 3, 4):
            ag_take(g, G, h)
        moved(
            tabs[g][G].at[pl.ds(0, 8 * COUNTS[G]), :], ag_send.at[g, G], sib_recv.at[g, G]
        ).wait_recv()

    def along_x(src, dst, G):
        @pl.loop(0, 8)
        def _(y):
            rows = [pl.ds(pl.multiple_of(64 * i + 8 * y, 8), 8) for i in range(8)]
            tiles = [src[G, rows[i], :] for i in range(8)]
            v = vel[0]
            for i in range(8):
                dst[G, rows[i], :] = tiles[i] + v * contract(lambda k: DERIV[i][k], tiles)

    def along_yz(src, dst, G):
        @pl.loop(0, 8)
        def _(i):
            rows = [pl.ds(pl.multiple_of(64 * i + 8 * y, 8), 8) for y in range(8)]
            tiles = [src[G, rows[y], :] for y in range(8)]
            v = vel[1]
            for y in range(8):
                dst[G, rows[y], :] += v * contract(lambda k: DERIV[y][k], tiles)
            cols = [pl.ds(64 * i + q, 8, stride=8) for q in range(8)]
            tiles = [src[G, cols[q], :] for q in range(8)]
            v = vel[2]
            for q in range(8):
                dst[G, cols[q], :] += v * contract(lambda k: DERIV[q][k], tiles)

    def lift(dst, G, value, scale):
        dst[G, 0:64, :] += scale * value(0)
        dst[G, 448:512, :] += scale * value(1)
        for f, o in ((2, 0), (3, 56)):
            rows = scale * value(f)
            for i in range(8):
                dst[G, 64 * i + o : 64 * i + o + 8, :] += rows[8 * i : 8 * i + 8]
        dst[G, pl.ds(0, 64, stride=8), :] += scale * value(4)
        dst[G, pl.ds(7, 64, stride=8), :] += scale * value(5)

    def advance(src, dst, G):
        along_x(src, dst, G)
        along_yz(src, dst, G)

        def own_face(f):
            return face_pair(src, G, f // 2)[64 * (f % 2) : 64 * (f % 2) + 64]

        lift(dst, G, own_face, -LIFT)

    def facing(g, G, dst, scale):
        table = tabs[g][G]

        @pl.loop(0, E // 2)
        def _(i):
            for k in range(2):
                e = 2 * i + k
                for f in range(6):
                    row = where[8 * (G // 2) + f, e]
                    gat[pl.ds(f * E + e, 1), :] = table[pl.ds(row, 1), :]

        def got(f):
            rows = gat[f * E : f * E + E, :]
            if G < 2:
                return rows
            return jnp.where(upper[f * E : f * E + E, :] > 0.5, pltpu.roll(rows, 64, 1), rows)

        low = low_half(48)
        for pair in range(3):
            first, second = got(2 * pair), got(2 * pair + 1)
            fr[pair, 0:48, :] = jnp.where(low, first, pltpu.roll(second, 64, 1))
            fr[pair, 48:96, :] = (
                jnp.where(low, pltpu.roll(first, 64, 1), second)
                if G < 2
                else jnp.zeros((48, 128), F32)
            )
            wt[128 * pair : 128 * pair + 128, :] = fr[pair].T
        lift(dst, G, lambda f: wt[64 * f : 64 * f + 64, :], scale)

    one, two, three = ORDER
    fr[:, 96:128, :] = jnp.zeros((3, 32, 128), F32)
    operand_copies[0].wait()
    for G in ORDER:
        load(G)
        publish(u, 0, G)
        if G == one:
            pl.semaphore_wait(barrier, 12)
        if G != three:
            ag_start(0, G)
    for copy in operand_copies[1:6]:
        copy.wait()

    lane = lax.broadcasted_iota(jnp.int32, (E, 128), 1)
    element = lax.broadcasted_iota(jnp.int32, (E, 128), 0)
    spread = ((lane == element) | (lane == element + E)).astype(F32)

    def over_lanes(rows):
        return jnp.dot(rows, spread, precision=lax.Precision.HIGHEST, preferred_element_type=F32)

    speeds = over_lanes(-STEP * vel_ref[...])
    block = block_ref[...]
    label = lax.rem(block, 4) * 64 + owner_ref[...] * 2 + block // 4
    names[...] = jnp.broadcast_to(over_lanes(label.astype(F32)), (8, 128))
    for d in range(3):
        vel[d] = jnp.broadcast_to(speeds[d : d + 1], (8, 128))
    for d in range(1, 4):
        pltpu.make_async_remote_copy(
            src_ref=names,
            dst_ref=names_in.at[d - 1],
            send_sem=name_send,
            recv_sem=name_recv,
            device_id=(z * 4 + lax.rem(x + d, 4), ax),
            device_id_type=MESH,
        ).start()

    row = nbv_ref[...]
    slot = row - ROWS
    device = slot // E
    slot = slot - E * device
    upper_row = (row >= ROWS) & (slot >= 24)
    where_v[0:6, 0:E] = row
    where_v[8:14, 0:E] = jnp.where(
        row < ROWS, row, ROWS + 24 * device + slot - jnp.where(upper_row, 24, 0)
    )
    where_copy = pltpu.make_async_copy(where_v, where, where_sem)
    where_copy.start()
    folds = upper_row.astype(F32)
    diagonal = lax.broadcasted_iota(jnp.int32, (E, E), 0) == lax.broadcasted_iota(
        jnp.int32, (E, E), 1
    )
    for f in range(6):
        upper[f * E : f * E + E, :] = jnp.dot(
            jnp.where(diagonal, folds[f : f + 1, :], 0.0),
            jnp.ones((E, 128), F32),
            preferred_element_type=F32,
        )

    def coef(which, out):
        return lambda k: mt[pl.ds(64 * which + 8 * out + k, 1), :]

    def sample(G):
        @pl.loop(0, 8)
        def _(y):
            rows = [pl.ds(pl.multiple_of(64 * i + 8 * y, 8), 8) for i in range(8)]
            tiles = [b[G, rows[i], :] for i in range(8)]
            for r in range(8):
                b2[rows[r], :] = contract(coef(1, r), tiles)

        @pl.loop(0, 8)
        def _(r):
            cols = [pl.ds(64 * r + q, 8, stride=8) for q in range(8)]
            tiles = [b2[cols[q], :] for q in range(8)]
            for q in range(8):
                a[G, cols[q], :] = contract(coef(2, q), tiles)

    def sample_half(G, half):
        @pl.loop(0, 4)
        def _(r):
            low = low_half(8)
            tiles = [
                [a[G, pl.ds(pl.multiple_of(64 * (r + 4 * r2) + 8 * i, 8), 8), :] for i in range(8)]
                for r2 in range(2)
            ]
            for t in range(4 * half, 4 * half + 4):
                both = [contract(coef(0, t), tiles[r2]) for r2 in range(2)]
                if G < 2:
                    for r2 in range(2):
                        xs[r, G, r2, 8 * t : 8 * t + 8, :] = both[r2]
                else:
                    xc[r, 8 * t : 8 * t + 8, :] = jnp.where(
                        low, both[0], pltpu.roll(both[1], 64, 1)
                    )

    def x_half(ref, G, half):
        rows = pl.ds(32 * half, 32)
        return ref.at[:, rows, :] if G < 2 else ref.at[rows, :]

    def x_from(G, d):
        return xr.at[G, d] if G < 2 else xrc.at[d]

    def x_to(G, d):
        return xs.at[d, G] if G < 2 else xc.at[d]

    def x_start(G, half):
        for d in (2, 1, 3):
            target = lax.rem(x + d, 4)
            pltpu.make_async_remote_copy(
                src_ref=x_half(x_to(G, target), G, half),
                dst_ref=x_half(x_from(G, d - 1), G, half),
                send_sem=x_send,
                recv_sem=x_recv.at[G, half],
                device_id=(z * 4 + target, ax),
                device_id_type=MESH,
            ).start()

    def set_places():
        moved(names_in, name_send, name_recv).wait_recv()
        rows = lax.broadcasted_iota(jnp.int32, (256, 128), 0)
        lanes = lax.broadcasted_iota(jnp.int32, (1, 128), 1)
        for s in range(4):
            name = (names[0:1, :] if s == 0 else names_in[s - 1, 0:1, :]).astype(jnp.int32)
            place[:, 128 * s : 128 * s + 128] = (rows == name).astype(F32).astype(BF16)
            name = jnp.where(
                lanes < 64, name, pltpu.roll(names[0:1, :] if s == 0 else names_in[s - 1, 0:1, :], 64, 1).astype(jnp.int32)
            )
            place_c[:, 128 * s : 128 * s + 128] = (rows == name).astype(F32).astype(BF16)

    low8 = low_half(8)

    def x_finish(G, half):
        rows = pl.ds(32 * half, 32)
        arrived = xr.at[G, :, :, rows] if G < 2 else xrc.at[:, rows]
        moved(arrived, x_send, x_recv.at[G, half]).wait_recv()
        sources = [x_half(x_to(G, x), G, half)] + [x_half(x_from(G, d), G, half) for d in range(3)]
        values = jnp.concatenate([v[...].reshape(-1, 128) for v in sources], axis=1)
        width = E if G < 2 else 64
        names_of = place if G < 2 else place_c
        wide = lax.rem(lax.broadcasted_iota(jnp.int32, values.shape, 1), 128)
        high = values.astype(BF16).astype(F32)
        part = 0.0
        for term in (high, values - high):
            stack = jnp.concatenate(
                [
                    jnp.where((wide >= width * k) & (wide < width * k + E), term, 0.0).astype(BF16)
                    for k in range(2)
                ],
                axis=0,
            )
            part = part + lax.dot_general(
                stack, names_of[...], (((1,), (1,)), ((), ())), preferred_element_type=F32
            )
        for c in range(FIELDS[G]):
            for r2 in range(2):
                for tp in range(2):
                    o = 64 * c + 32 * r2 + 16 * tp
                    for v in range(2):
                        even = part[o : o + 8, 128 * v : 128 * v + 128]
                        odd = part[o + 8 : o + 16, 128 * v : 128 * v + 128]
                        zs[4 * v + r2, G, half, c, tp] = jnp.where(
                            low8, even, pltpu.roll(odd, 64, 1)
                        )
                        zs[4 * v + 2 + r2, G, half, c, tp] = jnp.where(
                            low8, pltpu.roll(even, 64, 1), odd
                        )
        z_first(G, half)

    def z_copy(kind, k, G, half):
        reach, step = ((4, 2), (3, 1), (2, 2), (1, 1))[kind]
        way = (1, 7)[k]
        fields = pl.ds(0, FIELDS[G])
        return pltpu.make_async_remote_copy(
            src_ref=zs.at[lax.rem(z + way * reach, 8), G, half, fields],
            dst_ref=zr.at[G, half, k, kind, fields],
            send_sem=z_send,
            recv_sem=z_recv.at[G, half, k] if kind < 2 else z_last.at[G, half],
            device_id=(lax.rem(z + way * step, 8) * 4 + x, ax),
            device_id_type=MESH,
        )

    def z_first(G, half):
        z_copy(0, half, G, half).start()
        for k in (half, 1 - half):
            z_copy(1, k, G, half).start()

    def z_second(G, half):
        fields = pl.ds(0, FIELDS[G])
        for k in (1 - half, half):
            target = lax.rem(z + (2, 6)[k], 8)
            least = 0 if k == half else 1
            moved(
                zr.at[G, half, k, pl.ds(least, 2 - least), fields], z_send, z_recv.at[G, half, k]
            ).wait_recv()
            more = zr[G, half, k, 1, fields]
            if k == half:
                more = more + zr[G, half, k, 0, fields]
            zs[target, G, half, fields] += more
            z_copy(2, k, G, half).start()
        for k in range(2):
            z_copy(3, k, G, half).start()

    def new_rows(G):
        width = E * FIELDS[G]
        for n in range(4):
            turned = b[G, 128 * n : 128 * n + 128, :].T
            new_ref[96 * G : 96 * G + width, 128 * n : 128 * n + 128] = turned[0:width]

    def first_section(G):
        facing(0, G, a, LIFT)
        publish(a, 1, G)
        ag_start(1, G)

    def second_base(G):
        advance(a, b, G)
        b[G] = 0.5 * (u[G] + b[G])

    def second_section(G):
        facing(1, G, b, 0.5 * LIFT)
        sample(G)
        for half in range(2):
            sample_half(G, half)
            x_start(G, half)

    advance(u, a, one)
    advance(u, a, two)
    ag_take(0, one, 2)
    ag_start(0, three)
    advance(u, a, three)
    where_copy.wait()
    ag_take(0, two, 2)
    ag_rest(0, one)
    first_section(one)
    ag_take(0, three, 2)
    ag_rest(0, two)
    first_section(two)
    mt[...] = over_lanes(maps_ref[...])
    second_base(one)
    ag_take(1, one, 2)
    ag_rest(0, three)
    first_section(three)
    second_base(two)
    ag_take(1, two, 2)
    set_places()
    ag_rest(1, one)
    second_section(one)
    second_base(three)
    ag_take(1, three, 2)
    ag_rest(1, two)
    second_section(two)
    x_finish(one, 0)
    x_finish(one, 1)
    ag_rest(1, three)
    second_section(three)
    z_second(one, 0)
    z_second(one, 1)
    x_finish(two, 0)
    x_finish(two, 1)
    for G in range(3):
        new_rows(G)
    x_finish(three, 0)
    z_second(two, 0)
    x_finish(three, 1)
    z_second(two, 1)
    z_second(three, 0)
    z_second(three, 1)
    for G in range(3):
        for half in range(2):
            moved(
                zr.at[G, half, :, pl.ds(2, 2), pl.ds(0, FIELDS[G])], z_send, z_last.at[G, half]
            ).wait_recv()
    for G in range(3):
        for half in range(2):
            for c in range(FIELDS[G]):
                total = zs[z, G, half, c]
                for kind in (3, 2):
                    for k in range(2):
                        total = total + zr[G, half, k, kind, c]
                for tp in range(2):
                    sum_ref[2 * half + tp, 2 * G + c] = total[tp]

    for copy in operand_copies[6:]:
        copy.wait()
    for g in range(2):
        for G in range(3):
            moved(
                tabs[g][G].at[pl.ds(0, 15 * COUNTS[G]), :], ag_send.at[g, G], sib_recv.at[g, G]
            ).wait_send()
    moved(names_in, name_send, name_recv).wait_send()
    for G in range(2):
        moved(xr.at[G], x_send, x_recv.at[0, 0]).wait_send()
    moved(xrc, x_send, x_recv.at[0, 0]).wait_send()
    for G in range(3):
        for half in range(2):
            fields = pl.ds(0, FIELDS[G])
            moved(
                zr.at[G, half, :, pl.ds(1, 3), fields], z_send, z_last.at[0, 0]
            ).wait_send()
            moved(zr.at[G, half, 0, 0, fields], z_send, z_last.at[0, 0]).wait_send()


def finish(
    rows_ref, sum_ref, table_ref, twiddle_ref, new_ref, spec_hbm, spec_ref, out_sem
):
    new_copy = pltpu.make_async_copy(rows_ref, new_ref, out_sem.at[0])
    new_copy.start()
    series = sum_ref[...].reshape(4 * C * 8, 128)
    high = series.astype(BF16)
    low = (series - high.astype(F32)).astype(BF16)
    points = (
        jnp.dot(high, table_ref[0], preferred_element_type=F32)
        + jnp.dot(low, table_ref[0], preferred_element_type=F32)
        + jnp.dot(high, table_ref[1], preferred_element_type=F32)
    )
    for v in range(4):
        real, imag = 0.0, 0.0
        for t in range(8):
            span = slice(8 * C * (t // 2), 8 * C * (t // 2) + 8 * C)
            re = points[span, 256 * (t % 2) : 256 * (t % 2) + 128]
            im = points[span, 256 * (t % 2) + 128 : 256 * (t % 2) + 256]
            wr = twiddle_ref[0, t : t + 1, 128 * v : 128 * v + 128]
            wi = twiddle_ref[1, t : t + 1, 128 * v : 128 * v + 128]
            real = real + (re * wr - im * wi)
            imag = imag + (re * wi + im * wr)
        spec_ref[0, :, 128 * v : 128 * v + 128] = real
        spec_ref[1, :, 128 * v : 128 * v + 128] = imag
    spec_copy = pltpu.make_async_copy(spec_ref, spec_hbm, out_sem.at[1])
    spec_copy.start()
    spec_copy.wait()
    new_copy.wait()


def per_device(n_ax, state, velocity, interp_maps, neighbours, send_faces, owner_device, owner_block):
    vmem = pl.BlockSpec(memory_space=pltpu.VMEM)
    hbm = pl.BlockSpec(memory_space=pl.ANY)
    dma = pltpu.SemaphoreType.DMA
    nodes = pltpu.VMEM((3, 512, 128), F32)
    handed = pl.pallas_call(
        functools.partial(kernel, n_ax),
        out_shape=(
            pltpu.VMEM((C * E, 512), F32),
            pltpu.VMEM((4, C, 8, 128), F32),
            pltpu.VMEM(TABLES.shape, BF16),
            pltpu.VMEM(TWIDDLE.shape, F32),
        ),
        in_specs=[hbm] * 9,
        out_specs=(vmem,) * 4,
        scratch_shapes=[
            pltpu.VMEM((3, 128, 512), F32),
            nodes,
            nodes,
            nodes,
            pltpu.VMEM((512, 128), F32),
            pltpu.VMEM((3, 8, 128), F32),
            pltpu.VMEM((192, 128), F32),
            pltpu.VMEM((3, 128, 128), F32),
            pltpu.VMEM((3, ROWS, 128), F32),
            pltpu.VMEM((E, 128), F32),
            *[pltpu.VMEM((ROWS + n * n_ax, 128), F32) for n in COUNTS * 2],
            pltpu.VMEM((ROWS, 128), F32),
            pltpu.VMEM((16, 128), jnp.int32),
            pltpu.SMEM((16, 128), jnp.int32),
            pltpu.VMEM((ROWS, 128), F32),
            pltpu.VMEM((3, E), F32),
            pltpu.VMEM((192, E), F32),
            pltpu.VMEM((1, E), jnp.int32),
            pltpu.VMEM((1, E), jnp.int32),
            pltpu.VMEM((6, E), jnp.int32),
            pltpu.SMEM((1, E), jnp.int32),
            pltpu.VMEM((384, 128), F32),
            pltpu.VMEM((8, 128), F32),
            pltpu.VMEM((3, 8, 128), F32),
            pltpu.VMEM((256, 512), BF16),
            pltpu.VMEM((256, 512), BF16),
            pltpu.VMEM((4, 2, 2, 64, 128), F32),
            pltpu.VMEM((4, 64, 128), F32),
            pltpu.VMEM((2, 3, 2, 64, 128), F32),
            pltpu.VMEM((3, 64, 128), F32),
            pltpu.VMEM((8, 3, 2, 2, 2, 8, 128), F32),
            pltpu.VMEM((3, 2, 2, 4, 2, 2, 8, 128), F32),
            dma((8,)),
            dma,
            dma((3,)),
            dma((2, 3)),
            dma((2, 3, 2, 4)),
            dma((2, 3)),
            dma,
            dma,
            dma,
            dma((3, 2)),
            dma,
            dma((3, 2, 2)),
            dma((3, 2)),
        ],
        compiler_params=pltpu.CompilerParams(
            collective_id=0, has_side_effects=True, vmem_limit_bytes=56 * 1024 * 1024
        ),
        name="advance",
    )(
        velocity.T,
        interp_maps.transpose(1, 2, 3, 0).reshape(192, E),
        owner_device.reshape(1, E),
        owner_block.reshape(1, E),
        neighbours.T,
        send_faces.reshape(1, E),
        state.transpose(1, 0, 2).reshape(C * E, 512),
        jnp.asarray(TABLES),
        jnp.asarray(TWIDDLE),
    )
    new, spec = pl.pallas_call(
        finish,
        out_shape=(
            jax.ShapeDtypeStruct((C * E, 512), F32),
            jax.ShapeDtypeStruct((2, 8 * C, 512), F32),
        ),
        in_specs=[vmem] * 4,
        out_specs=(hbm, hbm),
        scratch_shapes=[pltpu.VMEM((2, 8 * C, 512), F32), dma((2,))],
        name="spectra",
    )(*[pltpu.with_memory_space_constraint(array, pltpu.VMEM) for array in handed])
    return (
        new.reshape(C, E, 512).transpose(1, 0, 2),
        spec.reshape(2, C, 8, 512),
    )


def solution(mesh):
    return jax.shard_map(
        functools.partial(per_device, mesh.shape["ax"]),
        mesh=mesh,
        in_specs=(
            P(("az", "ax"), None, None),
            P(("az", "ax"), None),
            P(("az", "ax"), None, None, None),
            P(("az", "ax"), None),
            P(("az", "ax")),
            P(("az", "ax"), None),
            P(("az", "ax")),
        ),
        out_specs=(P(("az", "ax"), None, None), P(None, None, ("az", "ax"), None)),
        check_vma=False,
    )
```

```python
import functools

import jax
import jax.numpy as jnp
import ml_dtypes
import numpy as np
from jax import lax
from jax.experimental import pallas as pl
from jax.experimental.pallas import tpu as pltpu
from jax.sharding import PartitionSpec as P

MESH = pl.DeviceIdType.MESH
F32 = jnp.float32
BF16 = jnp.bfloat16
E = 48
C = 5
ROWS = 6 * E
COUNTS = (48, 48, 24)
RISING = (24, 24, 16)
FIELDS = (2, 2, 1)
ORDER = (2, 0, 1)
STEP = 0.02
LIFT = 0.02 * 5.0


def spectral_derivative():
    points = np.cos(np.pi * np.arange(8) / 7.0)
    ends = (np.arange(8) == 0) | (np.arange(8) == 7)
    scales = np.where(ends, 2.0, 1.0)
    signs = np.where(np.arange(8) % 2 == 0, 1.0, -1.0)
    differ = points[:, None] - points[None, :]
    offdiag = (
        scales[:, None]
        / scales[None, :]
        * signs[:, None]
        * signs[None, :]
        / np.where(np.eye(8) > 0, 1.0, differ)
    )
    inner = -points / (2.0 * np.where(ends, 1.0, 1.0 - points * points))
    corner = (2.0 * 49.0 + 1.0) / 6.0
    diagonal = np.where(np.arange(8) == 0, corner, np.where(np.arange(8) == 7, -corner, inner))
    return np.where(np.eye(8) > 0, diagonal[:, None], offdiag)


DERIV = [[float(np.float32(v)) for v in row] for row in spectral_derivative()]


def dft_tables():
    j, m0 = np.meshgrid(np.arange(64), np.arange(64), indexing="ij")
    angle = (j * m0 % 64) * (2.0 * np.pi / 64)
    points = np.concatenate([np.cos(angle)] * 2 + [-np.sin(angle)] * 2, axis=1)
    table = np.zeros((2, 64, 2, 256))
    table[0, :, 0], table[1, :, 1] = points, points
    table = table.reshape(128, 512)
    high = table.astype(ml_dtypes.bfloat16)
    low = (table - high.astype(np.float64)).astype(ml_dtypes.bfloat16)
    t, m = np.meshgrid(np.arange(8), np.arange(512), indexing="ij")
    angle = (t * m % 512) * (2.0 * np.pi / 512)
    twiddle = np.stack([np.cos(angle), -np.sin(angle)]) * 512**-0.5
    return np.stack([high, low]), twiddle.astype(np.float32)


TABLES, TWIDDLE = dft_tables()


def contract(coef, tiles):
    total = coef(0) * tiles[0]
    for k in range(1, len(tiles)):
        total = total + coef(k) * tiles[k]
    return total


def kernel(
    n_ax,
    vel_hbm,
    maps_hbm,
    owner_hbm,
    block_hbm,
    nbv_hbm,
    send_hbm,
    state_ref,
    table_hbm,
    twiddle_hbm,
    new_ref,
    sum_ref,
    table_ref,
    twiddle_ref,
    flat,
    u,
    a,
    b,
    b2,
    vel,
    mt,
    fr,
    local,
    last,
    tab_a0,
    tab_b0,
    tab_c0,
    tab_a1,
    tab_b1,
    tab_c1,
    gat,
    where_v,
    where,
    upper,
    vel_ref,
    maps_ref,
    owner_ref,
    block_ref,
    nbv_ref,
    send_ref,
    wt,
    names,
    names_in,
    place,
    place_c,
    xs,
    xc,
    xr,
    xrc,
    zs,
    zr,
    in_sem,
    where_sem,
    state_sem,
    ag_send,
    y_recv,
    sib_recv,
    name_send,
    name_recv,
    x_send,
    x_recv,
    z_send,
    z_recv,
    z_last,
):
    az, ax = lax.axis_index("az"), lax.axis_index("ax")
    z, x = az // 4, az % 4
    up, dn = lax.rem(ax + 2, n_ax), lax.rem(ax + n_ax - 2, n_ax)
    up2, dn2 = lax.rem(ax + 4, n_ax), lax.rem(ax + n_ax - 4, n_ax)
    sib = ax + 1 - 2 * lax.rem(ax, 2)
    tabs = ((tab_a0, tab_b0, tab_c0), (tab_a1, tab_b1, tab_c1))

    state_copies = [
        pltpu.make_async_copy(
            state_ref.at[pl.ds(96 * G, E * FIELDS[G])],
            flat.at[G, pl.ds(0, E * FIELDS[G])],
            state_sem.at[G],
        )
        for G in range(3)
    ]
    operand_copies = [
        pltpu.make_async_copy(src, dst, in_sem.at[n])
        for n, (src, dst) in enumerate(
            (
                (send_hbm, send_ref),
                (vel_hbm, vel_ref),
                (owner_hbm, owner_ref),
                (block_hbm, block_ref),
                (nbv_hbm, nbv_ref),
                (maps_hbm, maps_ref),
                (table_hbm, table_ref),
                (twiddle_hbm, twiddle_ref),
            )
        )
    ]
    for copy in state_copies + operand_copies:
        copy.start()
    barrier = pltpu.get_barrier_semaphore()
    for peer in (up, dn, up2, dn2, sib):
        pl.semaphore_signal(barrier, inc=1, device_id=(az, peer), device_id_type=MESH)
    for d in range(1, 4):
        pl.semaphore_signal(
            barrier, inc=1, device_id=(z * 4 + lax.rem(x + d, 4), ax), device_id_type=MESH
        )
    for d in (1, 2, 6, 7):
        pl.semaphore_signal(
            barrier, inc=1, device_id=(lax.rem(z + d, 8) * 4 + x, ax), device_id_type=MESH
        )

    def low_half(rows):
        return lax.broadcasted_iota(jnp.int32, (rows, 128), 1) < 64

    def moved(ref, send, recv):
        return pltpu.make_async_remote_copy(
            src_ref=ref,
            dst_ref=ref,
            send_sem=send,
            recv_sem=recv,
            device_id=(az, sib),
            device_id_type=MESH,
        )

    def load(G):
        width = E * FIELDS[G]
        flat[G, width:128] = jnp.zeros((128 - width, 512), F32)
        state_copies[G].wait()
        for n in range(4):
            u[G, 128 * n : 128 * n + 128, :] = flat[G, :, 128 * n : 128 * n + 128].T

    def face_pair(ref, G, pair):
        if pair == 0:
            return jnp.concatenate([ref[G, 0:64, :], ref[G, 448:512, :]], axis=0)
        if pair == 1:
            return jnp.concatenate(
                [ref[G, 64 * i + o : 64 * i + o + 8, :] for o in (0, 56) for i in range(8)], axis=0
            )
        return jnp.concatenate(
            [ref[G, pl.ds(0, 64, stride=8), :], ref[G, pl.ds(7, 64, stride=8), :]], axis=0
        )

    def publish(ref, g, G):
        table = tabs[g][G]
        low = low_half(48)
        for pair in range(3):
            turned = face_pair(ref, G, pair).T
            first = turned[0:48]
            second = turned[48:96]
            even = jnp.where(low, first, pltpu.roll(second, 64, 1))
            odd = jnp.where(low, pltpu.roll(first, 64, 1), second)
            for o, rows in ((0, even), (1, odd)):
                f = 2 * pair + o
                local[G, pl.ds(f, 48, stride=6), :] = rows
                table[pl.ds(f, 48, stride=6), :] = rows
        own = pl.multiple_of(ROWS + COUNTS[G] * ax, 8)

        @pl.loop(0, 6)
        def _(i):
            for k in range(8):
                s = 8 * i + k
                row = local[G, pl.ds(send_ref[0, s], 1), :]
                if G < 2:
                    table[pl.ds(own + s, 1), :] = row
                else:
                    last[pl.ds(s, 1), :] = row

        if G == 2:
            table[pl.ds(own, 24), :] = jnp.where(
                low_half(24), last[0:24, :], pltpu.roll(last[24:48, :], 64, 1)
            )

    def ag_copy(g, source, G, part, target, recv):
        start, count = 0, COUNTS[G]
        if part == 0:
            count = RISING[G]
        if part == 1:
            start, count = RISING[G], COUNTS[G] - RISING[G]
        rows = pl.ds(pl.multiple_of(ROWS + COUNTS[G] * source + start, 8), count)
        return pltpu.make_async_remote_copy(
            src_ref=tabs[g][G].at[rows, :],
            dst_ref=tabs[g][G].at[rows, :],
            send_sem=ag_send.at[g, G],
            recv_sem=recv,
            device_id=(az, target),
            device_id_type=MESH,
        )

    def behind(way, h):
        return lax.rem(ax + (n_ax - 2 * h if way == 0 else 2 * h), n_ax)

    WHOLE = 2
    ways = ((0, up, up2), (1, dn, dn2))

    def share(g, source, G, part):
        ag_copy(g, source, G, part, sib, sib_recv.at[g, G]).start()

    def ag_start(g, G):
        for way, _, two in ways:
            ag_copy(g, ax, G, WHOLE, two, y_recv.at[g, G, way, 1]).start()
        share(g, ax, G, WHOLE)

    def ag_near(g, G):
        for way, one, _ in ways:
            ag_copy(g, ax, G, WHOLE, one, y_recv.at[g, G, way, 0]).start()

    def ag_take(g, G, h):
        for way, one, two in ways:
            source = behind(way, h)
            part = WHOLE if h < 4 else way
            ag_copy(g, source, G, part, one, y_recv.at[g, G, way, h - 1]).wait_recv()
            if h == 2:
                ag_copy(g, source, G, way, two, y_recv.at[g, G, way, 3]).start()
                ag_copy(g, source, G, WHOLE, one, y_recv.at[g, G, way, 2]).start()
            share(g, source, G, part)

    def ag_rest(g, G):
        for h in (1, 3, 4):
            ag_take(g, G, h)
        moved(
            tabs[g][G].at[pl.ds(0, 8 * COUNTS[G]), :], ag_send.at[g, G], sib_recv.at[g, G]
        ).wait_recv()

    def along_x(src, dst, G):
        @pl.loop(0, 8)
        def _(y):
            rows = [pl.ds(pl.multiple_of(64 * i + 8 * y, 8), 8) for i in range(8)]
            tiles = [src[G, rows[i], :] for i in range(8)]
            v = vel[0]
            for i in range(8):
                dst[G, rows[i], :] = tiles[i] + v * contract(lambda k: DERIV[i][k], tiles)

    def along_yz(src, dst, G):
        @pl.loop(0, 8)
        def _(i):
            rows = [pl.ds(pl.multiple_of(64 * i + 8 * y, 8), 8) for y in range(8)]
            tiles = [src[G, rows[y], :] for y in range(8)]
            v = vel[1]
            for y in range(8):
                dst[G, rows[y], :] += v * contract(lambda k: DERIV[y][k], tiles)
            cols = [pl.ds(64 * i + q, 8, stride=8) for q in range(8)]
            tiles = [src[G, cols[q], :] for q in range(8)]
            v = vel[2]
            for q in range(8):
                dst[G, cols[q], :] += v * contract(lambda k: DERIV[q][k], tiles)

    def lift(dst, G, value, scale):
        dst[G, 0:64, :] += scale * value(0)
        dst[G, 448:512, :] += scale * value(1)
        for f, o in ((2, 0), (3, 56)):
            rows = scale * value(f)
            for i in range(8):
                dst[G, 64 * i + o : 64 * i + o + 8, :] += rows[8 * i : 8 * i + 8]
        dst[G, pl.ds(0, 64, stride=8), :] += scale * value(4)
        dst[G, pl.ds(7, 64, stride=8), :] += scale * value(5)

    def advance(src, dst, G):
        along_x(src, dst, G)
        along_yz(src, dst, G)

        def own_face(f):
            return face_pair(src, G, f // 2)[64 * (f % 2) : 64 * (f % 2) + 64]

        lift(dst, G, own_face, -LIFT)

    def facing(g, G, dst, scale):
        table = tabs[g][G]

        @pl.loop(0, E // 2)
        def _(i):
            for k in range(2):
                e = 2 * i + k
                for f in range(6):
                    row = where[8 * (G // 2) + f, e]
                    gat[pl.ds(f * E + e, 1), :] = table[pl.ds(row, 1), :]

        def got(f):
            rows = gat[f * E : f * E + E, :]
            if G < 2:
                return rows
            return jnp.where(upper[f * E : f * E + E, :] > 0.5, pltpu.roll(rows, 64, 1), rows)

        low = low_half(48)
        for pair in range(3):
            first, second = got(2 * pair), got(2 * pair + 1)
            fr[pair, 0:48, :] = jnp.where(low, first, pltpu.roll(second, 64, 1))
            fr[pair, 48:96, :] = (
                jnp.where(low, pltpu.roll(first, 64, 1), second)
                if G < 2
                else jnp.zeros((48, 128), F32)
            )
            wt[128 * pair : 128 * pair + 128, :] = fr[pair].T
        lift(dst, G, lambda f: wt[64 * f : 64 * f + 64, :], scale)

    one, two, three = ORDER
    fr[:, 96:128, :] = jnp.zeros((3, 32, 128), F32)
    operand_copies[0].wait()
    for G in ORDER:
        load(G)
        publish(u, 0, G)
        if G == one:
            pl.semaphore_wait(barrier, 12)
        if G != three:
            ag_start(0, G)
        if G == one:
            ag_near(0, one)
    for copy in operand_copies[1:6]:
        copy.wait()

    lane = lax.broadcasted_iota(jnp.int32, (E, 128), 1)
    element = lax.broadcasted_iota(jnp.int32, (E, 128), 0)
    spread = ((lane == element) | (lane == element + E)).astype(F32)

    def over_lanes(rows):
        return jnp.dot(rows, spread, precision=lax.Precision.HIGHEST, preferred_element_type=F32)

    speeds = over_lanes(-STEP * vel_ref[...])
    block = block_ref[...]
    label = lax.rem(block, 4) * 64 + owner_ref[...] * 2 + block // 4
    names[...] = jnp.broadcast_to(over_lanes(label.astype(F32)), (8, 128))
    for d in range(3):
        vel[d] = jnp.broadcast_to(speeds[d : d + 1], (8, 128))
    for d in range(1, 4):
        pltpu.make_async_remote_copy(
            src_ref=names,
            dst_ref=names_in.at[d - 1],
            send_sem=name_send,
            recv_sem=name_recv,
            device_id=(z * 4 + lax.rem(x + d, 4), ax),
            device_id_type=MESH,
        ).start()

    row = nbv_ref[...]
    slot = row - ROWS
    device = slot // E
    slot = slot - E * device
    upper_row = (row >= ROWS) & (slot >= 24)
    where_v[0:6, 0:E] = row
    where_v[8:14, 0:E] = jnp.where(
        row < ROWS, row, ROWS + 24 * device + slot - jnp.where(upper_row, 24, 0)
    )
    where_copy = pltpu.make_async_copy(where_v, where, where_sem)
    where_copy.start()
    folds = upper_row.astype(F32)
    diagonal = lax.broadcasted_iota(jnp.int32, (E, E), 0) == lax.broadcasted_iota(
        jnp.int32, (E, E), 1
    )
    for f in range(6):
        upper[f * E : f * E + E, :] = jnp.dot(
            jnp.where(diagonal, folds[f : f + 1, :], 0.0),
            jnp.ones((E, 128), F32),
            preferred_element_type=F32,
        )

    def coef(which, out):
        return lambda k: mt[pl.ds(64 * which + 8 * out + k, 1), :]

    def sample(G):
        @pl.loop(0, 8)
        def _(y):
            rows = [pl.ds(pl.multiple_of(64 * i + 8 * y, 8), 8) for i in range(8)]
            tiles = [b[G, rows[i], :] for i in range(8)]
            for r in range(8):
                b2[rows[r], :] = contract(coef(1, r), tiles)

        @pl.loop(0, 8)
        def _(r):
            cols = [pl.ds(64 * r + q, 8, stride=8) for q in range(8)]
            tiles = [b2[cols[q], :] for q in range(8)]
            for q in range(8):
                a[G, cols[q], :] = contract(coef(2, q), tiles)

    def sample_half(G, half):
        @pl.loop(0, 4)
        def _(r):
            low = low_half(8)
            tiles = [
                [a[G, pl.ds(pl.multiple_of(64 * (r + 4 * r2) + 8 * i, 8), 8), :] for i in range(8)]
                for r2 in range(2)
            ]
            for t in range(4 * half, 4 * half + 4):
                both = [contract(coef(0, t), tiles[r2]) for r2 in range(2)]
                if G < 2:
                    for r2 in range(2):
                        xs[r, G, r2, 8 * t : 8 * t + 8, :] = both[r2]
                else:
                    xc[r, 8 * t : 8 * t + 8, :] = jnp.where(
                        low, both[0], pltpu.roll(both[1], 64, 1)
                    )

    def x_half(ref, G, half):
        rows = pl.ds(32 * half, 32)
        return ref.at[:, rows, :] if G < 2 else ref.at[rows, :]

    def x_from(G, d):
        return xr.at[G, d] if G < 2 else xrc.at[d]

    def x_to(G, d):
        return xs.at[d, G] if G < 2 else xc.at[d]

    def x_start(G, half):
        for d in (2, 1, 3):
            target = lax.rem(x + d, 4)
            pltpu.make_async_remote_copy(
                src_ref=x_half(x_to(G, target), G, half),
                dst_ref=x_half(x_from(G, d - 1), G, half),
                send_sem=x_send,
                recv_sem=x_recv.at[G, half],
                device_id=(z * 4 + target, ax),
                device_id_type=MESH,
            ).start()

    def set_places():
        moved(names_in, name_send, name_recv).wait_recv()
        rows = lax.broadcasted_iota(jnp.int32, (256, 128), 0)
        lanes = lax.broadcasted_iota(jnp.int32, (1, 128), 1)
        for s in range(4):
            name = (names[0:1, :] if s == 0 else names_in[s - 1, 0:1, :]).astype(jnp.int32)
            place[:, 128 * s : 128 * s + 128] = (rows == name).astype(F32).astype(BF16)
            name = jnp.where(
                lanes < 64, name, pltpu.roll(names[0:1, :] if s == 0 else names_in[s - 1, 0:1, :], 64, 1).astype(jnp.int32)
            )
            place_c[:, 128 * s : 128 * s + 128] = (rows == name).astype(F32).astype(BF16)

    low8 = low_half(8)

    def x_finish(G, half):
        rows = pl.ds(32 * half, 32)
        arrived = xr.at[G, :, :, rows] if G < 2 else xrc.at[:, rows]
        moved(arrived, x_send, x_recv.at[G, half]).wait_recv()
        sources = [x_half(x_to(G, x), G, half)] + [x_half(x_from(G, d), G, half) for d in range(3)]
        values = jnp.concatenate([v[...].reshape(-1, 128) for v in sources], axis=1)
        width = E if G < 2 else 64
        names_of = place if G < 2 else place_c
        wide = lax.rem(lax.broadcasted_iota(jnp.int32, values.shape, 1), 128)
        high = values.astype(BF16).astype(F32)
        part = 0.0
        for term in (high, values - high):
            stack = jnp.concatenate(
                [
                    jnp.where((wide >= width * k) & (wide < width * k + E), term, 0.0).astype(BF16)
                    for k in range(2)
                ],
                axis=0,
            )
            part = part + lax.dot_general(
                stack, names_of[...], (((1,), (1,)), ((), ())), preferred_element_type=F32
            )
        for c in range(FIELDS[G]):
            for r2 in range(2):
                for tp in range(2):
                    o = 64 * c + 32 * r2 + 16 * tp
                    for v in range(2):
                        even = part[o : o + 8, 128 * v : 128 * v + 128]
                        odd = part[o + 8 : o + 16, 128 * v : 128 * v + 128]
                        zs[4 * v + r2, G, half, c, tp] = jnp.where(
                            low8, even, pltpu.roll(odd, 64, 1)
                        )
                        zs[4 * v + 2 + r2, G, half, c, tp] = jnp.where(
                            low8, pltpu.roll(even, 64, 1), odd
                        )
        z_first(G, half)

    def z_copy(kind, k, G, half):
        reach, step = ((4, 2), (3, 1), (2, 2), (1, 1))[kind]
        way = (1, 7)[k]
        fields = pl.ds(0, FIELDS[G])
        return pltpu.make_async_remote_copy(
            src_ref=zs.at[lax.rem(z + way * reach, 8), G, half, fields],
            dst_ref=zr.at[G, half, k, kind, fields],
            send_sem=z_send,
            recv_sem=z_recv.at[G, half, k] if kind < 2 else z_last.at[G, half],
            device_id=(lax.rem(z + way * step, 8) * 4 + x, ax),
            device_id_type=MESH,
        )

    def z_first(G, half):
        z_copy(0, half, G, half).start()
        for kind in (1, 3):
            for k in (half, 1 - half):
                z_copy(kind, k, G, half).start()

    def z_second(G, half):
        fields = pl.ds(0, FIELDS[G])
        for k in (1 - half, half):
            target = lax.rem(z + (2, 6)[k], 8)
            least = 0 if k == half else 1
            moved(
                zr.at[G, half, k, pl.ds(least, 2 - least), fields], z_send, z_recv.at[G, half, k]
            ).wait_recv()
            more = zr[G, half, k, 1, fields]
            if k == half:
                more = more + zr[G, half, k, 0, fields]
            zs[target, G, half, fields] += more
            z_copy(2, k, G, half).start()

    def new_rows(G):
        width = E * FIELDS[G]
        for n in range(4):
            turned = b[G, 128 * n : 128 * n + 128, :].T
            new_ref[96 * G : 96 * G + width, 128 * n : 128 * n + 128] = turned[0:width]

    def first_section(G):
        facing(0, G, a, LIFT)
        publish(a, 1, G)
        ag_start(1, G)

    def second_base(G):
        advance(a, b, G)
        b[G] = 0.5 * (u[G] + b[G])

    def second_section(G):
        facing(1, G, b, 0.5 * LIFT)
        sample(G)
        for half in range(2):
            sample_half(G, half)
            x_start(G, half)

    advance(u, a, one)
    advance(u, a, two)
    ag_take(0, one, 2)
    ag_start(0, three)
    advance(u, a, three)
    where_copy.wait()
    ag_take(0, two, 2)
    ag_near(0, two)
    ag_near(0, three)
    ag_rest(0, one)
    first_section(one)
    ag_take(0, three, 2)
    ag_near(1, one)
    ag_rest(0, two)
    first_section(two)
    mt[...] = over_lanes(maps_ref[...])
    second_base(one)
    ag_take(1, one, 2)
    ag_near(1, two)
    ag_rest(0, three)
    first_section(three)
    second_base(two)
    ag_take(1, two, 2)
    ag_near(1, three)
    set_places()
    ag_rest(1, one)
    second_section(one)
    second_base(three)
    ag_take(1, three, 2)
    ag_rest(1, two)
    second_section(two)
    x_finish(one, 0)
    x_finish(one, 1)
    ag_rest(1, three)
    second_section(three)
    z_second(one, 0)
    z_second(one, 1)
    x_finish(two, 0)
    x_finish(two, 1)
    for G in range(3):
        new_rows(G)
    x_finish(three, 0)
    z_second(two, 0)
    x_finish(three, 1)
    z_second(two, 1)
    z_second(three, 0)
    z_second(three, 1)
    for G in range(3):
        for half in range(2):
            moved(
                zr.at[G, half, :, pl.ds(2, 2), pl.ds(0, FIELDS[G])], z_send, z_last.at[G, half]
            ).wait_recv()
    for G in range(3):
        for half in range(2):
            for c in range(FIELDS[G]):
                total = zs[z, G, half, c]
                for kind in (3, 2):
                    for k in range(2):
                        total = total + zr[G, half, k, kind, c]
                for tp in range(2):
                    sum_ref[2 * half + tp, 2 * G + c] = total[tp]

    for copy in operand_copies[6:]:
        copy.wait()
    for g in range(2):
        for G in range(3):
            moved(
                tabs[g][G].at[pl.ds(0, 15 * COUNTS[G]), :], ag_send.at[g, G], sib_recv.at[g, G]
            ).wait_send()
    moved(names_in, name_send, name_recv).wait_send()
    for G in range(2):
        moved(xr.at[G], x_send, x_recv.at[0, 0]).wait_send()
    moved(xrc, x_send, x_recv.at[0, 0]).wait_send()
    for G in range(3):
        for half in range(2):
            fields = pl.ds(0, FIELDS[G])
            moved(
                zr.at[G, half, :, pl.ds(1, 3), fields], z_send, z_last.at[0, 0]
            ).wait_send()
            moved(zr.at[G, half, 0, 0, fields], z_send, z_last.at[0, 0]).wait_send()


def finish(
    rows_ref, sum_ref, table_ref, twiddle_ref, new_ref, spec_hbm, spec_ref, out_sem
):
    new_copy = pltpu.make_async_copy(rows_ref, new_ref, out_sem.at[0])
    new_copy.start()
    series = sum_ref[...].reshape(4 * C * 8, 128)
    high = series.astype(BF16)
    low = (series - high.astype(F32)).astype(BF16)
    points = (
        jnp.dot(high, table_ref[0], preferred_element_type=F32)
        + jnp.dot(low, table_ref[0], preferred_element_type=F32)
        + jnp.dot(high, table_ref[1], preferred_element_type=F32)
    )
    for v in range(4):
        real, imag = 0.0, 0.0
        for t in range(8):
            span = slice(8 * C * (t // 2), 8 * C * (t // 2) + 8 * C)
            re = points[span, 256 * (t % 2) : 256 * (t % 2) + 128]
            im = points[span, 256 * (t % 2) + 128 : 256 * (t % 2) + 256]
            wr = twiddle_ref[0, t : t + 1, 128 * v : 128 * v + 128]
            wi = twiddle_ref[1, t : t + 1, 128 * v : 128 * v + 128]
            real = real + (re * wr - im * wi)
            imag = imag + (re * wi + im * wr)
        spec_ref[0, :, 128 * v : 128 * v + 128] = real
        spec_ref[1, :, 128 * v : 128 * v + 128] = imag
    spec_copy = pltpu.make_async_copy(spec_ref, spec_hbm, out_sem.at[1])
    spec_copy.start()
    spec_copy.wait()
    new_copy.wait()


def per_device(n_ax, state, velocity, interp_maps, neighbours, send_faces, owner_device, owner_block):
    vmem = pl.BlockSpec(memory_space=pltpu.VMEM)
    hbm = pl.BlockSpec(memory_space=pl.ANY)
    dma = pltpu.SemaphoreType.DMA
    nodes = pltpu.VMEM((3, 512, 128), F32)
    handed = pl.pallas_call(
        functools.partial(kernel, n_ax),
        out_shape=(
            pltpu.VMEM((C * E, 512), F32),
            pltpu.VMEM((4, C, 8, 128), F32),
            pltpu.VMEM(TABLES.shape, BF16),
            pltpu.VMEM(TWIDDLE.shape, F32),
        ),
        in_specs=[hbm] * 9,
        out_specs=(vmem,) * 4,
        scratch_shapes=[
            pltpu.VMEM((3, 128, 512), F32),
            nodes,
            nodes,
            nodes,
            pltpu.VMEM((512, 128), F32),
            pltpu.VMEM((3, 8, 128), F32),
            pltpu.VMEM((192, 128), F32),
            pltpu.VMEM((3, 128, 128), F32),
            pltpu.VMEM((3, ROWS, 128), F32),
            pltpu.VMEM((E, 128), F32),
            *[pltpu.VMEM((ROWS + n * n_ax, 128), F32) for n in COUNTS * 2],
            pltpu.VMEM((ROWS, 128), F32),
            pltpu.VMEM((16, 128), jnp.int32),
            pltpu.SMEM((16, 128), jnp.int32),
            pltpu.VMEM((ROWS, 128), F32),
            pltpu.VMEM((3, E), F32),
            pltpu.VMEM((192, E), F32),
            pltpu.VMEM((1, E), jnp.int32),
            pltpu.VMEM((1, E), jnp.int32),
            pltpu.VMEM((6, E), jnp.int32),
            pltpu.SMEM((1, E), jnp.int32),
            pltpu.VMEM((384, 128), F32),
            pltpu.VMEM((8, 128), F32),
            pltpu.VMEM((3, 8, 128), F32),
            pltpu.VMEM((256, 512), BF16),
            pltpu.VMEM((256, 512), BF16),
            pltpu.VMEM((4, 2, 2, 64, 128), F32),
            pltpu.VMEM((4, 64, 128), F32),
            pltpu.VMEM((2, 3, 2, 64, 128), F32),
            pltpu.VMEM((3, 64, 128), F32),
            pltpu.VMEM((8, 3, 2, 2, 2, 8, 128), F32),
            pltpu.VMEM((3, 2, 2, 4, 2, 2, 8, 128), F32),
            dma((8,)),
            dma,
            dma((3,)),
            dma((2, 3)),
            dma((2, 3, 2, 4)),
            dma((2, 3)),
            dma,
            dma,
            dma,
            dma((3, 2)),
            dma,
            dma((3, 2, 2)),
            dma((3, 2)),
        ],
        compiler_params=pltpu.CompilerParams(
            collective_id=0, has_side_effects=True, vmem_limit_bytes=56 * 1024 * 1024
        ),
        name="advance",
    )(
        velocity.T,
        interp_maps.transpose(1, 2, 3, 0).reshape(192, E),
        owner_device.reshape(1, E),
        owner_block.reshape(1, E),
        neighbours.T,
        send_faces.reshape(1, E),
        state.transpose(1, 0, 2).reshape(C * E, 512),
        jnp.asarray(TABLES),
        jnp.asarray(TWIDDLE),
    )
    new, spec = pl.pallas_call(
        finish,
        out_shape=(
            jax.ShapeDtypeStruct((C * E, 512), F32),
            jax.ShapeDtypeStruct((2, 8 * C, 512), F32),
        ),
        in_specs=[vmem] * 4,
        out_specs=(hbm, hbm),
        scratch_shapes=[pltpu.VMEM((2, 8 * C, 512), F32), dma((2,))],
        name="spectra",
    )(*[pltpu.with_memory_space_constraint(array, pltpu.VMEM) for array in handed])
    return (
        new.reshape(C, E, 512).transpose(1, 0, 2),
        spec.reshape(2, C, 8, 512),
    )


def solution(mesh):
    return jax.shard_map(
        functools.partial(per_device, mesh.shape["ax"]),
        mesh=mesh,
        in_specs=(
            P(("az", "ax"), None, None),
            P(("az", "ax"), None),
            P(("az", "ax"), None, None, None),
            P(("az", "ax"), None),
            P(("az", "ax")),
            P(("az", "ax"), None),
            P(("az", "ax")),
        ),
        out_specs=(P(("az", "ax"), None, None), P(None, None, ("az", "ax"), None)),
        check_vma=False,
    )
```

```python
import functools

import jax
import jax.numpy as jnp
import ml_dtypes
import numpy as np
from jax import lax
from jax.experimental import pallas as pl
from jax.experimental.pallas import tpu as pltpu
from jax.sharding import PartitionSpec as P

MESH = pl.DeviceIdType.MESH
F32 = jnp.float32
BF16 = jnp.bfloat16
E = 48
C = 5
ROWS = 6 * E
COUNTS = (48, 48, 24)
RISING = (24, 24, 16)
FIELDS = (2, 2, 1)
ORDER = (2, 0, 1)
STEP = 0.02
LIFT = 0.02 * 5.0


def spectral_derivative():
    points = np.cos(np.pi * np.arange(8) / 7.0)
    ends = (np.arange(8) == 0) | (np.arange(8) == 7)
    scales = np.where(ends, 2.0, 1.0)
    signs = np.where(np.arange(8) % 2 == 0, 1.0, -1.0)
    differ = points[:, None] - points[None, :]
    offdiag = (
        scales[:, None]
        / scales[None, :]
        * signs[:, None]
        * signs[None, :]
        / np.where(np.eye(8) > 0, 1.0, differ)
    )
    inner = -points / (2.0 * np.where(ends, 1.0, 1.0 - points * points))
    corner = (2.0 * 49.0 + 1.0) / 6.0
    diagonal = np.where(np.arange(8) == 0, corner, np.where(np.arange(8) == 7, -corner, inner))
    return np.where(np.eye(8) > 0, diagonal[:, None], offdiag)


DERIV = [[float(np.float32(v)) for v in row] for row in spectral_derivative()]


def dft_tables():
    j, m0 = np.meshgrid(np.arange(64), np.arange(64), indexing="ij")
    angle = (j * m0 % 64) * (2.0 * np.pi / 64)
    points = np.concatenate([np.cos(angle)] * 2 + [-np.sin(angle)] * 2, axis=1)
    table = np.zeros((2, 64, 2, 256))
    table[0, :, 0], table[1, :, 1] = points, points
    table = table.reshape(128, 512)
    high = table.astype(ml_dtypes.bfloat16)
    low = (table - high.astype(np.float64)).astype(ml_dtypes.bfloat16)
    t, m = np.meshgrid(np.arange(8), np.arange(512), indexing="ij")
    angle = (t * m % 512) * (2.0 * np.pi / 512)
    twiddle = np.stack([np.cos(angle), -np.sin(angle)]) * 512**-0.5
    return np.stack([high, low]), twiddle.astype(np.float32)


TABLES, TWIDDLE = dft_tables()


def contract(coef, tiles):
    total = coef(0) * tiles[0]
    for k in range(1, len(tiles)):
        total = total + coef(k) * tiles[k]
    return total


def kernel(
    n_ax,
    vel_hbm,
    maps_hbm,
    owner_hbm,
    block_hbm,
    nbv_hbm,
    send_hbm,
    state_ref,
    table_hbm,
    twiddle_hbm,
    new_ref,
    sum_ref,
    table_ref,
    twiddle_ref,
    flat,
    u,
    a,
    b,
    b2,
    vel,
    mt,
    fr,
    local,
    last,
    tab_a0,
    tab_b0,
    tab_c0,
    tab_a1,
    tab_b1,
    tab_c1,
    gat,
    where_v,
    where,
    upper,
    vel_ref,
    maps_ref,
    owner_ref,
    block_ref,
    nbv_ref,
    send_ref,
    wt,
    names,
    names_in,
    place,
    place_c,
    xs,
    xc,
    xr,
    xrc,
    zs,
    zr,
    in_sem,
    where_sem,
    state_sem,
    ag_send,
    y_recv,
    sib_recv,
    name_send,
    name_recv,
    x_send,
    x_recv,
    z_send,
    z_recv,
    z_last,
):
    az, ax = lax.axis_index("az"), lax.axis_index("ax")
    z, x = az // 4, az % 4
    up, dn = lax.rem(ax + 2, n_ax), lax.rem(ax + n_ax - 2, n_ax)
    up2, dn2 = lax.rem(ax + 4, n_ax), lax.rem(ax + n_ax - 4, n_ax)
    sib = ax + 1 - 2 * lax.rem(ax, 2)
    tabs = ((tab_a0, tab_b0, tab_c0), (tab_a1, tab_b1, tab_c1))

    state_copies = [
        pltpu.make_async_copy(
            state_ref.at[pl.ds(96 * G, E * FIELDS[G])],
            flat.at[G, pl.ds(0, E * FIELDS[G])],
            state_sem.at[G],
        )
        for G in range(3)
    ]
    operand_copies = [
        pltpu.make_async_copy(src, dst, in_sem.at[n])
        for n, (src, dst) in enumerate(
            (
                (send_hbm, send_ref),
                (vel_hbm, vel_ref),
                (owner_hbm, owner_ref),
                (block_hbm, block_ref),
                (nbv_hbm, nbv_ref),
                (maps_hbm, maps_ref),
                (table_hbm, table_ref),
                (twiddle_hbm, twiddle_ref),
            )
        )
    ]
    for copy in state_copies + operand_copies:
        copy.start()
    barrier = pltpu.get_barrier_semaphore()
    for peer in (up, dn, up2, dn2, sib):
        pl.semaphore_signal(barrier, inc=1, device_id=(az, peer), device_id_type=MESH)
    for d in range(1, 4):
        pl.semaphore_signal(
            barrier, inc=1, device_id=(z * 4 + lax.rem(x + d, 4), ax), device_id_type=MESH
        )
    for d in (1, 2, 6, 7):
        pl.semaphore_signal(
            barrier, inc=1, device_id=(lax.rem(z + d, 8) * 4 + x, ax), device_id_type=MESH
        )

    def low_half(rows):
        return lax.broadcasted_iota(jnp.int32, (rows, 128), 1) < 64

    def moved(ref, send, recv):
        return pltpu.make_async_remote_copy(
            src_ref=ref,
            dst_ref=ref,
            send_sem=send,
            recv_sem=recv,
            device_id=(az, sib),
            device_id_type=MESH,
        )

    def load(G):
        width = E * FIELDS[G]
        flat[G, width:128] = jnp.zeros((128 - width, 512), F32)
        state_copies[G].wait()
        for n in range(4):
            u[G, 128 * n : 128 * n + 128, :] = flat[G, :, 128 * n : 128 * n + 128].T

    def face_pair(ref, G, pair):
        if pair == 0:
            return jnp.concatenate([ref[G, 0:64, :], ref[G, 448:512, :]], axis=0)
        if pair == 1:
            return jnp.concatenate(
                [ref[G, 64 * i + o : 64 * i + o + 8, :] for o in (0, 56) for i in range(8)], axis=0
            )
        return jnp.concatenate(
            [ref[G, pl.ds(0, 64, stride=8), :], ref[G, pl.ds(7, 64, stride=8), :]], axis=0
        )

    def publish(ref, g, G):
        table = tabs[g][G]
        low = low_half(48)
        for pair in range(3):
            turned = face_pair(ref, G, pair).T
            first = turned[0:48]
            second = turned[48:96]
            even = jnp.where(low, first, pltpu.roll(second, 64, 1))
            odd = jnp.where(low, pltpu.roll(first, 64, 1), second)
            for o, rows in ((0, even), (1, odd)):
                f = 2 * pair + o
                local[G, pl.ds(f, 48, stride=6), :] = rows
                table[pl.ds(f, 48, stride=6), :] = rows
        own = pl.multiple_of(ROWS + COUNTS[G] * ax, 8)

        @pl.loop(0, 6)
        def _(i):
            for k in range(8):
                s = 8 * i + k
                row = local[G, pl.ds(send_ref[0, s], 1), :]
                if G < 2:
                    table[pl.ds(own + s, 1), :] = row
                else:
                    last[pl.ds(s, 1), :] = row

        if G == 2:
            table[pl.ds(own, 24), :] = jnp.where(
                low_half(24), last[0:24, :], pltpu.roll(last[24:48, :], 64, 1)
            )

    def ag_copy(g, source, G, part, target, recv):
        start, count = 0, COUNTS[G]
        if part == 0:
            count = RISING[G]
        if part == 1:
            start, count = RISING[G], COUNTS[G] - RISING[G]
        rows = pl.ds(pl.multiple_of(ROWS + COUNTS[G] * source + start, 8), count)
        return pltpu.make_async_remote_copy(
            src_ref=tabs[g][G].at[rows, :],
            dst_ref=tabs[g][G].at[rows, :],
            send_sem=ag_send.at[g, G],
            recv_sem=recv,
            device_id=(az, target),
            device_id_type=MESH,
        )

    def behind(way, h):
        return lax.rem(ax + (n_ax - 2 * h if way == 0 else 2 * h), n_ax)

    WHOLE = 2
    ways = ((0, up, up2), (1, dn, dn2))

    def share(g, source, G, part):
        ag_copy(g, source, G, part, sib, sib_recv.at[g, G]).start()

    def ag_start(g, G):
        for way, _, two in ways:
            ag_copy(g, ax, G, WHOLE, two, y_recv.at[g, G, way, 1]).start()
        share(g, ax, G, WHOLE)

    def ag_near(g, G):
        for way, one, _ in ways:
            ag_copy(g, ax, G, WHOLE, one, y_recv.at[g, G, way, 0]).start()

    def ag_take(g, G, h):
        for way, one, two in ways:
            source = behind(way, h)
            part = WHOLE if h < 4 else way
            ag_copy(g, source, G, part, one, y_recv.at[g, G, way, h - 1]).wait_recv()
            if h == 2:
                ag_copy(g, source, G, way, two, y_recv.at[g, G, way, 3]).start()
                ag_copy(g, source, G, WHOLE, one, y_recv.at[g, G, way, 2]).start()
            share(g, source, G, part)

    def ag_rest(g, G):
        for h in (1, 3, 4):
            ag_take(g, G, h)
        moved(
            tabs[g][G].at[pl.ds(0, 8 * COUNTS[G]), :], ag_send.at[g, G], sib_recv.at[g, G]
        ).wait_recv()

    def along_x(src, dst, G):
        @pl.loop(0, 8)
        def _(y):
            rows = [pl.ds(pl.multiple_of(64 * i + 8 * y, 8), 8) for i in range(8)]
            tiles = [src[G, rows[i], :] for i in range(8)]
            v = vel[0]
            for i in range(8):
                dst[G, rows[i], :] = tiles[i] + v * contract(lambda k: DERIV[i][k], tiles)

    def along_yz(src, dst, G):
        @pl.loop(0, 8)
        def _(i):
            rows = [pl.ds(pl.multiple_of(64 * i + 8 * y, 8), 8) for y in range(8)]
            tiles = [src[G, rows[y], :] for y in range(8)]
            v = vel[1]
            for y in range(8):
                dst[G, rows[y], :] += v * contract(lambda k: DERIV[y][k], tiles)
            cols = [pl.ds(64 * i + q, 8, stride=8) for q in range(8)]
            tiles = [src[G, cols[q], :] for q in range(8)]
            v = vel[2]
            for q in range(8):
                dst[G, cols[q], :] += v * contract(lambda k: DERIV[q][k], tiles)

    def lift(dst, G, value, scale):
        dst[G, 0:64, :] += scale * value(0)
        dst[G, 448:512, :] += scale * value(1)
        for f, o in ((2, 0), (3, 56)):
            rows = scale * value(f)
            for i in range(8):
                dst[G, 64 * i + o : 64 * i + o + 8, :] += rows[8 * i : 8 * i + 8]
        dst[G, pl.ds(0, 64, stride=8), :] += scale * value(4)
        dst[G, pl.ds(7, 64, stride=8), :] += scale * value(5)

    def advance(src, dst, G):
        along_x(src, dst, G)
        along_yz(src, dst, G)

        def own_face(f):
            return face_pair(src, G, f // 2)[64 * (f % 2) : 64 * (f % 2) + 64]

        lift(dst, G, own_face, -LIFT)

    def facing(g, G, dst, scale):
        table = tabs[g][G]

        @pl.loop(0, E // 2)
        def _(i):
            for k in range(2):
                e = 2 * i + k
                for f in range(6):
                    row = where[8 * (G // 2) + f, e]
                    gat[pl.ds(f * E + e, 1), :] = table[pl.ds(row, 1), :]

        def got(f):
            rows = gat[f * E : f * E + E, :]
            if G < 2:
                return rows
            return jnp.where(upper[f * E : f * E + E, :] > 0.5, pltpu.roll(rows, 64, 1), rows)

        low = low_half(48)
        for pair in range(3):
            first, second = got(2 * pair), got(2 * pair + 1)
            fr[pair, 0:48, :] = jnp.where(low, first, pltpu.roll(second, 64, 1))
            fr[pair, 48:96, :] = (
                jnp.where(low, pltpu.roll(first, 64, 1), second)
                if G < 2
                else jnp.zeros((48, 128), F32)
            )
            wt[128 * pair : 128 * pair + 128, :] = fr[pair].T
        lift(dst, G, lambda f: wt[64 * f : 64 * f + 64, :], scale)

    one, two, three = ORDER
    fr[:, 96:128, :] = jnp.zeros((3, 32, 128), F32)
    operand_copies[0].wait()
    for G in ORDER:
        load(G)
        publish(u, 0, G)
        if G == one:
            pl.semaphore_wait(barrier, 12)
        if G != three:
            ag_start(0, G)
        if G == one:
            ag_near(0, one)
    for copy in operand_copies[1:6]:
        copy.wait()

    lane = lax.broadcasted_iota(jnp.int32, (E, 128), 1)
    element = lax.broadcasted_iota(jnp.int32, (E, 128), 0)
    spread = ((lane == element) | (lane == element + E)).astype(F32)

    def over_lanes(rows):
        return jnp.dot(rows, spread, precision=lax.Precision.HIGHEST, preferred_element_type=F32)

    speeds = over_lanes(-STEP * vel_ref[...])
    block = block_ref[...]
    label = lax.rem(block, 4) * 64 + owner_ref[...] * 2 + block // 4
    names[...] = jnp.broadcast_to(over_lanes(label.astype(F32)), (8, 128))
    for d in range(3):
        vel[d] = jnp.broadcast_to(speeds[d : d + 1], (8, 128))
    for d in range(1, 4):
        pltpu.make_async_remote_copy(
            src_ref=names,
            dst_ref=names_in.at[d - 1],
            send_sem=name_send,
            recv_sem=name_recv,
            device_id=(z * 4 + lax.rem(x + d, 4), ax),
            device_id_type=MESH,
        ).start()

    row = nbv_ref[...]
    slot = row - ROWS
    device = slot // E
    slot = slot - E * device
    upper_row = (row >= ROWS) & (slot >= 24)
    where_v[0:6, 0:E] = row
    where_v[8:14, 0:E] = jnp.where(
        row < ROWS, row, ROWS + 24 * device + slot - jnp.where(upper_row, 24, 0)
    )
    where_copy = pltpu.make_async_copy(where_v, where, where_sem)
    where_copy.start()
    folds = upper_row.astype(F32)
    diagonal = lax.broadcasted_iota(jnp.int32, (E, E), 0) == lax.broadcasted_iota(
        jnp.int32, (E, E), 1
    )
    for f in range(6):
        upper[f * E : f * E + E, :] = jnp.dot(
            jnp.where(diagonal, folds[f : f + 1, :], 0.0),
            jnp.ones((E, 128), F32),
            preferred_element_type=F32,
        )

    def coef(which, out):
        return lambda k: mt[pl.ds(64 * which + 8 * out + k, 1), :]

    def sample(G):
        @pl.loop(0, 8)
        def _(y):
            rows = [pl.ds(pl.multiple_of(64 * i + 8 * y, 8), 8) for i in range(8)]
            tiles = [b[G, rows[i], :] for i in range(8)]
            for r in range(8):
                b2[rows[r], :] = contract(coef(1, r), tiles)

        @pl.loop(0, 8)
        def _(r):
            cols = [pl.ds(64 * r + q, 8, stride=8) for q in range(8)]
            tiles = [b2[cols[q], :] for q in range(8)]
            for q in range(8):
                a[G, cols[q], :] = contract(coef(2, q), tiles)

    def sample_half(G, half):
        @pl.loop(0, 4)
        def _(r):
            low = low_half(8)
            tiles = [
                [a[G, pl.ds(pl.multiple_of(64 * (r + 4 * r2) + 8 * i, 8), 8), :] for i in range(8)]
                for r2 in range(2)
            ]
            for t in range(4 * half, 4 * half + 4):
                both = [contract(coef(0, t), tiles[r2]) for r2 in range(2)]
                if G < 2:
                    for r2 in range(2):
                        xs[r, G, r2, 8 * t : 8 * t + 8, :] = both[r2]
                else:
                    xc[r, 8 * t : 8 * t + 8, :] = jnp.where(
                        low, both[0], pltpu.roll(both[1], 64, 1)
                    )

    def x_half(ref, G, half):
        rows = pl.ds(32 * half, 32)
        return ref.at[:, rows, :] if G < 2 else ref.at[rows, :]

    def x_from(G, d):
        return xr.at[G, d] if G < 2 else xrc.at[d]

    def x_to(G, d):
        return xs.at[d, G] if G < 2 else xc.at[d]

    def x_start(G, half):
        for d in (2, 1, 3):
            target = lax.rem(x + d, 4)
            pltpu.make_async_remote_copy(
                src_ref=x_half(x_to(G, target), G, half),
                dst_ref=x_half(x_from(G, d - 1), G, half),
                send_sem=x_send,
                recv_sem=x_recv.at[G, half],
                device_id=(z * 4 + target, ax),
                device_id_type=MESH,
            ).start()

    def set_places():
        moved(names_in, name_send, name_recv).wait_recv()
        rows = lax.broadcasted_iota(jnp.int32, (256, 128), 0)
        lanes = lax.broadcasted_iota(jnp.int32, (1, 128), 1)
        for s in range(4):
            name = (names[0:1, :] if s == 0 else names_in[s - 1, 0:1, :]).astype(jnp.int32)
            place[:, 128 * s : 128 * s + 128] = (rows == name).astype(F32).astype(BF16)
            name = jnp.where(
                lanes < 64, name, pltpu.roll(names[0:1, :] if s == 0 else names_in[s - 1, 0:1, :], 64, 1).astype(jnp.int32)
            )
            place_c[:, 128 * s : 128 * s + 128] = (rows == name).astype(F32).astype(BF16)

    low8 = low_half(8)

    def x_finish(G, half):
        rows = pl.ds(32 * half, 32)
        arrived = xr.at[G, :, :, rows] if G < 2 else xrc.at[:, rows]
        moved(arrived, x_send, x_recv.at[G, half]).wait_recv()
        sources = [x_half(x_to(G, x), G, half)] + [x_half(x_from(G, d), G, half) for d in range(3)]
        values = jnp.concatenate([v[...].reshape(-1, 128) for v in sources], axis=1)
        width = E if G < 2 else 64
        names_of = place if G < 2 else place_c
        wide = lax.rem(lax.broadcasted_iota(jnp.int32, values.shape, 1), 128)
        high = values.astype(BF16).astype(F32)
        part = 0.0
        for term in (high, values - high):
            stack = jnp.concatenate(
                [
                    jnp.where((wide >= width * k) & (wide < width * k + E), term, 0.0).astype(BF16)
                    for k in range(2)
                ],
                axis=0,
            )
            part = part + lax.dot_general(
                stack, names_of[...], (((1,), (1,)), ((), ())), preferred_element_type=F32
            )
        for c in range(FIELDS[G]):
            for r2 in range(2):
                for tp in range(2):
                    o = 64 * c + 32 * r2 + 16 * tp
                    for v in range(2):
                        even = part[o : o + 8, 128 * v : 128 * v + 128]
                        odd = part[o + 8 : o + 16, 128 * v : 128 * v + 128]
                        zs[4 * v + r2, G, half, c, tp] = jnp.where(
                            low8, even, pltpu.roll(odd, 64, 1)
                        )
                        zs[4 * v + 2 + r2, G, half, c, tp] = jnp.where(
                            low8, pltpu.roll(even, 64, 1), odd
                        )
        z_first(G, half)

    def z_copy(kind, k, G, half):
        reach, step = ((4, 2), (3, 1), (2, 2), (1, 1))[kind]
        way = (1, 7)[k]
        fields = pl.ds(0, FIELDS[G])
        return pltpu.make_async_remote_copy(
            src_ref=zs.at[lax.rem(z + way * reach, 8), G, half, fields],
            dst_ref=zr.at[G, half, k, kind, fields],
            send_sem=z_send,
            recv_sem=z_recv.at[G, half, k] if kind < 2 else z_last.at[G, half],
            device_id=(lax.rem(z + way * step, 8) * 4 + x, ax),
            device_id_type=MESH,
        )

    def z_first(G, half):
        z_copy(0, half, G, half).start()
        for kind in (1, 3):
            for k in (half, 1 - half):
                z_copy(kind, k, G, half).start()

    def z_second(G, half):
        fields = pl.ds(0, FIELDS[G])
        for k in (1 - half, half):
            target = lax.rem(z + (2, 6)[k], 8)
            least = 0 if k == half else 1
            moved(
                zr.at[G, half, k, pl.ds(least, 2 - least), fields], z_send, z_recv.at[G, half, k]
            ).wait_recv()
            more = zr[G, half, k, 1, fields]
            if k == half:
                more = more + zr[G, half, k, 0, fields]
            zs[target, G, half, fields] += more
            z_copy(2, k, G, half).start()

    def new_rows(G):
        width = E * FIELDS[G]
        for n in range(4):
            turned = b[G, 128 * n : 128 * n + 128, :].T
            new_ref[96 * G : 96 * G + width, 128 * n : 128 * n + 128] = turned[0:width]

    def first_section(G):
        facing(0, G, a, LIFT)
        publish(a, 1, G)
        ag_start(1, G)

    def second_base(G):
        advance(a, b, G)
        b[G] = 0.5 * (u[G] + b[G])

    def second_section(G):
        facing(1, G, b, 0.5 * LIFT)
        sample(G)
        for half in range(2):
            sample_half(G, half)
            x_start(G, half)

    advance(u, a, one)
    advance(u, a, two)
    ag_take(0, one, 2)
    ag_start(0, three)
    advance(u, a, three)
    where_copy.wait()
    ag_take(0, two, 2)
    ag_near(0, two)
    ag_near(0, three)
    ag_rest(0, one)
    first_section(one)
    ag_take(0, three, 2)
    ag_near(1, one)
    ag_rest(0, two)
    first_section(two)
    mt[...] = over_lanes(maps_ref[...])
    second_base(one)
    ag_take(1, one, 2)
    ag_near(1, two)
    ag_rest(0, three)
    first_section(three)
    second_base(two)
    ag_take(1, two, 2)
    ag_near(1, three)
    set_places()
    ag_rest(1, one)
    second_section(one)
    ag_take(1, three, 2)
    second_base(three)
    ag_rest(1, two)
    second_section(two)
    x_finish(one, 0)
    x_finish(one, 1)
    ag_rest(1, three)
    second_section(three)
    z_second(one, 0)
    z_second(one, 1)
    x_finish(two, 0)
    x_finish(two, 1)
    for G in range(3):
        new_rows(G)
    x_finish(three, 0)
    z_second(two, 0)
    x_finish(three, 1)
    z_second(two, 1)
    z_second(three, 0)
    z_second(three, 1)
    for G in range(3):
        for half in range(2):
            moved(
                zr.at[G, half, :, pl.ds(2, 2), pl.ds(0, FIELDS[G])], z_send, z_last.at[G, half]
            ).wait_recv()
    for G in range(3):
        for half in range(2):
            for c in range(FIELDS[G]):
                total = zs[z, G, half, c]
                for kind in (3, 2):
                    for k in range(2):
                        total = total + zr[G, half, k, kind, c]
                for tp in range(2):
                    sum_ref[2 * half + tp, 2 * G + c] = total[tp]

    for copy in operand_copies[6:]:
        copy.wait()
    for g in range(2):
        for G in range(3):
            moved(
                tabs[g][G].at[pl.ds(0, 15 * COUNTS[G]), :], ag_send.at[g, G], sib_recv.at[g, G]
            ).wait_send()
    moved(names_in, name_send, name_recv).wait_send()
    for G in range(2):
        moved(xr.at[G], x_send, x_recv.at[0, 0]).wait_send()
    moved(xrc, x_send, x_recv.at[0, 0]).wait_send()
    for G in range(3):
        for half in range(2):
            fields = pl.ds(0, FIELDS[G])
            moved(
                zr.at[G, half, :, pl.ds(1, 3), fields], z_send, z_last.at[0, 0]
            ).wait_send()
            moved(zr.at[G, half, 0, 0, fields], z_send, z_last.at[0, 0]).wait_send()


def finish(
    rows_ref, sum_ref, table_ref, twiddle_ref, new_ref, spec_hbm, spec_ref, out_sem
):
    new_copy = pltpu.make_async_copy(rows_ref, new_ref, out_sem.at[0])
    new_copy.start()
    series = sum_ref[...].reshape(4 * C * 8, 128)
    high = series.astype(BF16)
    low = (series - high.astype(F32)).astype(BF16)
    points = (
        jnp.dot(high, table_ref[0], preferred_element_type=F32)
        + jnp.dot(low, table_ref[0], preferred_element_type=F32)
        + jnp.dot(high, table_ref[1], preferred_element_type=F32)
    )
    for v in range(4):
        real, imag = 0.0, 0.0
        for t in range(8):
            span = slice(8 * C * (t // 2), 8 * C * (t // 2) + 8 * C)
            re = points[span, 256 * (t % 2) : 256 * (t % 2) + 128]
            im = points[span, 256 * (t % 2) + 128 : 256 * (t % 2) + 256]
            wr = twiddle_ref[0, t : t + 1, 128 * v : 128 * v + 128]
            wi = twiddle_ref[1, t : t + 1, 128 * v : 128 * v + 128]
            real = real + (re * wr - im * wi)
            imag = imag + (re * wi + im * wr)
        spec_ref[0, :, 128 * v : 128 * v + 128] = real
        spec_ref[1, :, 128 * v : 128 * v + 128] = imag
    spec_copy = pltpu.make_async_copy(spec_ref, spec_hbm, out_sem.at[1])
    spec_copy.start()
    spec_copy.wait()
    new_copy.wait()


def per_device(n_ax, state, velocity, interp_maps, neighbours, send_faces, owner_device, owner_block):
    vmem = pl.BlockSpec(memory_space=pltpu.VMEM)
    hbm = pl.BlockSpec(memory_space=pl.ANY)
    dma = pltpu.SemaphoreType.DMA
    nodes = pltpu.VMEM((3, 512, 128), F32)
    handed = pl.pallas_call(
        functools.partial(kernel, n_ax),
        out_shape=(
            pltpu.VMEM((C * E, 512), F32),
            pltpu.VMEM((4, C, 8, 128), F32),
            pltpu.VMEM(TABLES.shape, BF16),
            pltpu.VMEM(TWIDDLE.shape, F32),
        ),
        in_specs=[hbm] * 9,
        out_specs=(vmem,) * 4,
        scratch_shapes=[
            pltpu.VMEM((3, 128, 512), F32),
            nodes,
            nodes,
            nodes,
            pltpu.VMEM((512, 128), F32),
            pltpu.VMEM((3, 8, 128), F32),
            pltpu.VMEM((192, 128), F32),
            pltpu.VMEM((3, 128, 128), F32),
            pltpu.VMEM((3, ROWS, 128), F32),
            pltpu.VMEM((E, 128), F32),
            *[pltpu.VMEM((ROWS + n * n_ax, 128), F32) for n in COUNTS * 2],
            pltpu.VMEM((ROWS, 128), F32),
            pltpu.VMEM((16, 128), jnp.int32),
            pltpu.SMEM((16, 128), jnp.int32),
            pltpu.VMEM((ROWS, 128), F32),
            pltpu.VMEM((3, E), F32),
            pltpu.VMEM((192, E), F32),
            pltpu.VMEM((1, E), jnp.int32),
            pltpu.VMEM((1, E), jnp.int32),
            pltpu.VMEM((6, E), jnp.int32),
            pltpu.SMEM((1, E), jnp.int32),
            pltpu.VMEM((384, 128), F32),
            pltpu.VMEM((8, 128), F32),
            pltpu.VMEM((3, 8, 128), F32),
            pltpu.VMEM((256, 512), BF16),
            pltpu.VMEM((256, 512), BF16),
            pltpu.VMEM((4, 2, 2, 64, 128), F32),
            pltpu.VMEM((4, 64, 128), F32),
            pltpu.VMEM((2, 3, 2, 64, 128), F32),
            pltpu.VMEM((3, 64, 128), F32),
            pltpu.VMEM((8, 3, 2, 2, 2, 8, 128), F32),
            pltpu.VMEM((3, 2, 2, 4, 2, 2, 8, 128), F32),
            dma((8,)),
            dma,
            dma((3,)),
            dma((2, 3)),
            dma((2, 3, 2, 4)),
            dma((2, 3)),
            dma,
            dma,
            dma,
            dma((3, 2)),
            dma,
            dma((3, 2, 2)),
            dma((3, 2)),
        ],
        compiler_params=pltpu.CompilerParams(
            collective_id=0, has_side_effects=True, vmem_limit_bytes=56 * 1024 * 1024
        ),
        name="advance",
    )(
        velocity.T,
        interp_maps.transpose(1, 2, 3, 0).reshape(192, E),
        owner_device.reshape(1, E),
        owner_block.reshape(1, E),
        neighbours.T,
        send_faces.reshape(1, E),
        state.transpose(1, 0, 2).reshape(C * E, 512),
        jnp.asarray(TABLES),
        jnp.asarray(TWIDDLE),
    )
    new, spec = pl.pallas_call(
        finish,
        out_shape=(
            jax.ShapeDtypeStruct((C * E, 512), F32),
            jax.ShapeDtypeStruct((2, 8 * C, 512), F32),
        ),
        in_specs=[vmem] * 4,
        out_specs=(hbm, hbm),
        scratch_shapes=[pltpu.VMEM((2, 8 * C, 512), F32), dma((2,))],
        name="spectra",
    )(*[pltpu.with_memory_space_constraint(array, pltpu.VMEM) for array in handed])
    return (
        new.reshape(C, E, 512).transpose(1, 0, 2),
        spec.reshape(2, C, 8, 512),
    )


def solution(mesh):
    return jax.shard_map(
        functools.partial(per_device, mesh.shape["ax"]),
        mesh=mesh,
        in_specs=(
            P(("az", "ax"), None, None),
            P(("az", "ax"), None),
            P(("az", "ax"), None, None, None),
            P(("az", "ax"), None),
            P(("az", "ax")),
            P(("az", "ax"), None),
            P(("az", "ax")),
        ),
        out_specs=(P(("az", "ax"), None, None), P(None, None, ("az", "ax"), None)),
        check_vma=False,
    )
```
